128 devices in a mesh: dp: 2 (over y_hi), ctx: 16 (over z, y_lo, core), tp: 4 (over x).
Axes of the slice: x: 4, y: 4 (y_hi: 2, y_lo: 2; y = y_hi * 2 + y_lo), z: 4, core: 2. Of those that a mesh axis runs over, the one named last changes fastest.
Arguments:
- activations: bfloat16 [16384, 5120], P(('dp', 'ctx')), parts along dimension 0, may hold values from -48 to 48
- residual: bfloat16 [16384, 5120], P(('dp', 'ctx', 'tp')), parts along dimension 0, may hold values from -1.5 to 1.5
- w_query: bfloat16 [5120, 2560], P(None, 'tp'), may hold values from -0.078125 to 0.078125
- w_key: bfloat16 [5120, 512], P(None, 'tp'), may hold values from -0.078125 to 0.078125
- w_value: bfloat16 [5120, 512], P(None, 'tp'), may hold values from -0.078125 to 0.078125
- w_out: bfloat16 [2560, 5120], P('tp'), may hold values from -0.47265625 to 0.47265625
- gain: float32 [5120], replicated, may hold values from 0.5 to 1.5
- ancestors: int32 [128, 16], P(('dp', 'ctx')), parts along dimension 0, may hold values from -1 to 62, as said below
- kept: int32 [128], P(('dp', 'ctx')), parts along dimension 0, may hold values 0 or 1
Outputs:
- normed_out: bfloat16 [16384, 5120], P(('dp', 'ctx', 'tp')), parts along dimension 0
The draws below stay inside these ranges and needn't reach their ends.
There are 2 independent parts, one for each index of `dp`. The reference program is written for one: setup_inputs(seed, part) draws one part's arguments, and reference() takes and returns one part's arrays. A program takes and returns all parts, laid end to end along the dimension named above; an argument that names none is the same for every part. Nothing has to cross between parts.
Inputs may be any that keep to these rules, and one draw needn't show every extreme that they name: Entry l of a block's list is its ancestor block at depth l, earlier in the order; the list holds as many entries as the block's depth and -1 after them; some block has a full list; blocks 0 to 7 are ancestors of every later block.
All inputs are finite; a program needn't handle non-finite values. No bound on the sum of `kept` on one device may be relied on, other than what follows from the above.
Results may differ from the reference program's by a relative error of at most 0.015.
The reference program's roundings to bfloat16 on the way (of `queries`, `prob_bf` and `head_out`) count: a program that leaves them out, or rounds other values in their place, can miss the bound.
Values may be sent and summed in bfloat16 or wider, within the bound.
No kernel may reach another device: no remote copies, remote signals or barrier semaphores. Data moves between devices by JAX's collectives and lax.ppermute only.
A program may use at most 256 MiB of HBM per device.

```python
import math
import jax
import jax.numpy as jnp
from jax import lax

D = 5120
HEADS = 20
KVH = 4
HD = 128
BLK = 128
TOKENS = 8192
NBLK = 64
MAXANC = 16
N_TP = 4


def draw_ancestors(key, part):
    nblocks = TOKENS // BLK
    deepest = MAXANC
    floor_level = deepest // 2
    coin_key, back_key = jax.random.split(key)
    coin_flips = jax.random.randint(coin_key, (nblocks,), 0, 2)
    back_draws = jax.random.randint(back_key, (nblocks,), 0, 1 << 20)
    levels = jnp.arange(deepest + 1, dtype=jnp.int32)

    def advance(running, inputs):
        cur_depth, latest = running
        block_index, coin_flip, back_draw = inputs
        climb = jnp.minimum(cur_depth + 1, deepest)
        spread = jnp.maximum(cur_depth - floor_level + 1, 1)
        back_depth = floor_level + back_draw % spread
        chosen = jnp.where(coin_flip == 1, climb, back_depth)
        chosen = jnp.where(block_index == nblocks - 2, floor_level, chosen)
        chosen = jnp.where(block_index == nblocks - 1, floor_level + 1, chosen)
        new_depth = jnp.where(block_index <= deepest, block_index, chosen).astype(jnp.int32)
        anc_row = jnp.where(levels[:deepest] < new_depth, latest[:deepest], -1).astype(jnp.int32)
        latest = jnp.where(levels == new_depth, block_index, latest).astype(jnp.int32)
        return ((new_depth, latest), anc_row)
    start_state = (jnp.int32(0), jnp.full((deepest + 1,), -1, jnp.int32))
    inputs = (jnp.arange(nblocks, dtype=jnp.int32), coin_flips.astype(jnp.int32), back_draws.astype(jnp.int32))
    _, anc_rows = lax.scan(advance, start_state, inputs)
    return anc_rows


def draw_activations(key, part):
    base_key = jax.random.fold_in(key, 0)
    values = jnp.clip(jax.random.normal(base_key, (TOKENS, D), jnp.float32), -4.0, 4.0)
    return values.astype(jnp.bfloat16)


def with_ends(array, rng, smallest, top_value):
    shape = array.shape
    index_at = [jax.random.randint(jax.random.fold_in(rng, axis), (), 0, shape[axis]) for axis in range(len(shape))]
    array = array.at[tuple(index_at)].set(smallest)
    longest = shape.index(max(shape))
    index_at[longest] = (index_at[longest] + 1) % shape[longest]
    return array.at[tuple(index_at)].set(top_value)


def block_levels(rng, extent, shards, smallest, high):
    level = 1.0
    for axis_at, parts in shards:
        draws = jax.random.uniform(jax.random.fold_in(jax.random.fold_in(rng, 6), axis_at), (parts,), jnp.float32, smallest / len(shards), high / len(shards))
        level = level * jnp.repeat(jnp.exp(draws), extent[axis_at] // parts).reshape((-1,) + (1,) * (len(extent) - 1 - axis_at))
    return level


def centred(stream_key, extent, scale, reach, cuts=(), kind=jnp.bfloat16):
    values = scale * jax.random.normal(stream_key, extent, jnp.float32)
    if cuts:
        values = values * block_levels(stream_key, extent, cuts, -0.22, 0.18)
    return jnp.clip(values, -reach, reach).astype(kind)


def setup_inputs(seed: int = 0, part: int = 0) -> dict:
    arg_keys = jax.random.split(jax.random.key(seed), 10)
    part_keys = jax.random.split(jax.random.fold_in(arg_keys[9], part), 10)
    return {
        "activations": draw_activations(jax.random.fold_in(jax.random.fold_in(arg_keys[9], part), 71), part),
        "residual": centred(part_keys[1], (TOKENS, D), 0.25, 1.5, ((0, 64),)),
        "w_query": centred(arg_keys[2], (D, HEADS * HD), D ** -0.5, 0.078125, ((1, 4),)),
        "w_key": centred(arg_keys[3], (D, KVH * HD), D ** -0.5, 0.078125, ((1, 4),)),
        "w_value": centred(arg_keys[4], (D, KVH * HD), D ** -0.5, 0.078125, ((1, 4),)),
        "w_out": centred(arg_keys[5], (HEADS * HD, D), (4.0 / (HEADS * HD) ** 0.5), 0.47265625, ((0, 4),)),
        "gain": jnp.clip(1.0 + 0.1 * jax.random.normal(arg_keys[6], (D,), jnp.float32), 0.5, 1.5),
        "ancestors": draw_ancestors(jax.random.fold_in(jax.random.fold_in(arg_keys[9], part), 71), part),
        "kept": with_ends((jax.random.randint(part_keys[8], (NBLK,), 0, 2) < 1).astype(jnp.int32), jax.random.fold_in(part_keys[8], 1), 0, 1),
    }


def attend(query_block, key_block, value_block, listed_ok):
    slot_count = listed_ok.shape[0]
    blk_rows = query_block.shape[0]
    score_scale = 1.0 / math.sqrt(query_block.shape[-1])
    scores = jnp.einsum('qkgd,nkd->kgqn', query_block.astype(jnp.float32), key_block.astype(jnp.float32)) * score_scale
    column = jnp.arange(slot_count * blk_rows, dtype=jnp.int32)
    own_cols = column >= (slot_count - 1) * blk_rows
    offset = column - (slot_count - 1) * blk_rows
    row_ids = jnp.arange(blk_rows, dtype=jnp.int32)
    allowed = jnp.repeat(listed_ok, blk_rows)[None, :] & (jnp.logical_not(own_cols)[None, :] | (offset[None, :] <= row_ids[:, None]))
    scores = jnp.where(allowed, scores, -jnp.inf)
    row_max = lax.optimization_barrier(jnp.max(scores, axis=-1, keepdims=True))
    weights = jnp.where(allowed, jnp.exp(scores - row_max), 0.0)
    row_total = lax.optimization_barrier(jnp.sum(weights, axis=-1, keepdims=True))
    prob_bf = weights.astype(jnp.bfloat16)
    summed = jnp.einsum('kgqn,nkd->qkgd', prob_bf.astype(jnp.float32), value_block.astype(jnp.float32))
    return summed / jnp.transpose(row_total, (2, 0, 1, 3))

def reference(activations, residual, w_query, w_key, w_value, w_out, gain, ancestors, kept):
    group_size = HEADS // KVH
    nblocks = TOKENS // BLK
    queries = jnp.dot(activations, w_query, preferred_element_type=jnp.float32).astype(jnp.bfloat16)
    key_rows = jnp.dot(activations, w_key, preferred_element_type=jnp.float32).astype(jnp.bfloat16)
    value_rows = jnp.dot(activations, w_value, preferred_element_type=jnp.float32).astype(jnp.bfloat16)
    query_blocks = queries.reshape(nblocks, BLK, KVH, group_size, HD)
    key_blocks = key_rows.reshape(nblocks, BLK, KVH, HD)
    value_blocks = value_rows.reshape(nblocks, BLK, KVH, HD)
    own_ids = jnp.arange(nblocks, dtype=jnp.int32)
    key_lists = jnp.concatenate([ancestors.astype(jnp.int32), own_ids[:, None]], axis=1)

    def one_block(block_pair):
        query_block, id_list = block_pair
        listed_ok = id_list >= 0
        safe_ids = jnp.maximum(id_list, 0)
        chosen_keys = key_blocks[safe_ids].reshape(-1, KVH, HD)
        chosen_values = value_blocks[safe_ids].reshape(-1, KVH, HD)
        return attend(query_block, chosen_keys, chosen_values, listed_ok)
    attended = lax.map(one_block, (query_blocks, key_lists))
    head_out = attended.astype(jnp.bfloat16).reshape(TOKENS, HEADS * HD)
    head_cols = HEADS * HD // N_TP
    projected = jnp.zeros((TOKENS, D), jnp.float32)
    for shard in range(N_TP):
        term = jnp.dot(head_out[:, shard * head_cols:(shard + 1) * head_cols], w_out[shard * head_cols:(shard + 1) * head_cols], preferred_element_type=jnp.float32)
        rounded = lax.optimization_barrier(term.astype(jnp.bfloat16))
        projected = projected + rounded.astype(jnp.float32)
    mixed_rows = residual.astype(jnp.float32) + projected
    mean_square = lax.optimization_barrier(jnp.mean(mixed_rows * mixed_rows, axis=-1, keepdims=True))
    keep_rows = jnp.repeat(kept, BLK).astype(jnp.float32)
    normed = mixed_rows * lax.rsqrt(mean_square + 1e-06) * gain[None, :] * keep_rows[:, None]
    return normed.astype(jnp.bfloat16)
```

```python
import math

import jax
import jax.numpy as jnp
from jax import lax
from jax.experimental import pallas as pl
from jax.experimental.pallas import tpu as pltpu
from jax.sharding import Mesh, PartitionSpec as P

HD = 128
BLK = 128
CHUNK = 4
CTX = ("z", "y", "core")
F32 = jnp.float32
BF16 = jnp.bfloat16
SCALE2 = math.log2(math.e) / math.sqrt(HD)
NT = (((1,), (1,)), ((), ()))


def kv_kernel(x_ref, wk_ref, wv_ref, o_ref, acc_ref):
    step = pl.program_id(0)

    @pl.when(step == 0)
    def _():
        acc_ref[...] = jnp.zeros_like(acc_ref)

    w = jnp.concatenate([wk_ref[...], wv_ref[...]], axis=1)
    acc_ref[...] += jnp.dot(x_ref[...], w, preferred_element_type=F32)

    @pl.when(step == pl.num_programs(0) - 1)
    def _():
        o_ref[...] = acc_ref[...].astype(BF16)


def kv_project(x, wk, wv):
    rows, depth = x.shape
    tile = 640
    return pl.pallas_call(
        kv_kernel,
        name="kv_project",
        out_shape=jax.ShapeDtypeStruct((rows, 2 * HD), BF16),
        grid=(depth // tile,),
        in_specs=[
            pl.BlockSpec((rows, tile), lambda k: (0, k)),
            pl.BlockSpec((tile, HD), lambda k: (k, 0)),
            pl.BlockSpec((tile, HD), lambda k: (k, 0)),
        ],
        out_specs=pl.BlockSpec((rows, 2 * HD), lambda k: (0, 0)),
        scratch_shapes=[pltpu.VMEM((rows, 2 * HD), F32)],
        cost_estimate=pl.CostEstimate(
            flops=2 * rows * depth * 2 * HD,
            bytes_accessed=2 * depth * (rows + 2 * HD),
            transcendentals=0,
        ),
    )(x, wk, wv)


def block_kernel(
    meta_ref, anc_ref, q_ref, kv_ref, w_ref, o_ref,
    kvbuf, kvown, wbuf, sbuf, mbuf, lbuf, abuf, sems, wsem,
):
    local, own = meta_ref[0], meta_ref[1]
    slots = anc_ref.shape[1]
    heads = q_ref.shape[1] // HD
    wide = CHUNK * BLK

    own_copy = pltpu.make_async_copy(
        kv_ref.at[pl.ds(pl.multiple_of(own * BLK, BLK), BLK)], kvown, sems.at[slots]
    )
    own_copy.start()
    count = jnp.int32(0)
    for l in range(slots):
        entry = anc_ref[local, l]
        count += jnp.where(entry >= 0, 1, 0).astype(jnp.int32)
        src = pl.multiple_of(jnp.maximum(entry, 0) * BLK, BLK)
        pltpu.make_async_copy(
            kv_ref.at[pl.ds(src, BLK)], kvbuf.at[pl.ds(l * BLK, BLK)], sems.at[l]
        ).start()
    w_copy = pltpu.make_async_copy(w_ref, wbuf, wsem.at[0])
    w_copy.start()

    q_all = q_ref[...]
    q = jnp.concatenate([q_all[:, h * HD:(h + 1) * HD] for h in range(heads)], axis=0)
    own_copy.wait()
    s_own = lax.dot_general(q, kvown[:, :HD], NT, preferred_element_type=F32)
    row = lax.broadcasted_iota(jnp.int32, s_own.shape, 0) % BLK
    col = lax.broadcasted_iota(jnp.int32, s_own.shape, 1)
    s_own = jnp.where(col <= row, s_own, -jnp.inf)
    mbuf[...] = s_own
    for l in range(slots):
        pltpu.make_async_copy(
            kv_ref.at[pl.ds(0, BLK)], kvbuf.at[pl.ds(l * BLK, BLK)], sems.at[l]
        ).wait()
    chunks = (count + CHUNK - 1) // CHUNK

    def score(c, _):
        base = pl.multiple_of(c * wide, wide)
        s = lax.dot_general(q, kvbuf[pl.ds(base, wide), :HD], NT, preferred_element_type=F32)
        m = mbuf[...]
        for j in range(CHUNK):
            piece = s[:, j * BLK:(j + 1) * BLK]
            piece = jnp.where(c * CHUNK + j < count, piece, -jnp.inf)
            sbuf[c, :, j * BLK:(j + 1) * BLK] = piece
            m = jnp.maximum(m, piece)
        mbuf[...] = m
        return 0

    lax.fori_loop(0, chunks, score, 0)
    m = jnp.max(mbuf[...], axis=1, keepdims=True)
    p = jnp.exp2((s_own - m) * SCALE2)
    lbuf[...] = p
    abuf[...] = jnp.dot(p.astype(BF16), kvown[:, HD:], preferred_element_type=F32)

    def weigh(c, _):
        base = pl.multiple_of(c * wide, wide)
        w = jnp.exp2((sbuf[c] - m) * SCALE2)
        total = lbuf[...]
        for j in range(CHUNK):
            total += w[:, j * BLK:(j + 1) * BLK]
        lbuf[...] = total
        abuf[...] += jnp.dot(
            w.astype(BF16), kvbuf[pl.ds(base, wide), HD:], preferred_element_type=F32
        )
        return 0

    lax.fori_loop(0, chunks, weigh, 0)
    total = jnp.sum(lbuf[...], axis=1, keepdims=True)
    out = (abuf[...] / total).astype(BF16)
    head_out = jnp.concatenate([out[h * BLK:(h + 1) * BLK] for h in range(heads)], axis=1)
    w_copy.wait()
    cols = w_ref.shape[1]
    step = 1280
    for c in range(0, cols, step):
        o_ref[:, c:c + step] = jnp.dot(
            head_out, wbuf[:, c:c + step], preferred_element_type=F32
        ).astype(BF16)


def block_term(meta, anc, q, kv, w_out):
    slots = anc.shape[1]
    width = q.shape[1]
    rows = BLK * (width // HD)
    cols = w_out.shape[1]
    keys = (slots + 1) * BLK
    return pl.pallas_call(
        block_kernel,
        name="block_term",
        out_shape=jax.ShapeDtypeStruct((BLK, cols), BF16),
        grid_spec=pltpu.PrefetchScalarGridSpec(
            num_scalar_prefetch=2,
            grid=(1,),
            in_specs=[
                pl.BlockSpec((BLK, width), lambda i, meta, anc: (meta[0], 0)),
                pl.BlockSpec(memory_space=pl.ANY),
                pl.BlockSpec(memory_space=pl.ANY),
            ],
            out_specs=pl.BlockSpec((BLK, cols), lambda i, meta, anc: (0, 0)),
            scratch_shapes=[
                pltpu.VMEM((slots * BLK, 2 * HD), BF16),
                pltpu.VMEM((BLK, 2 * HD), BF16),
                pltpu.VMEM(w_out.shape, BF16),
                pltpu.VMEM((slots // CHUNK, rows, CHUNK * BLK), F32),
                pltpu.VMEM((rows, BLK), F32),
                pltpu.VMEM((rows, BLK), F32),
                pltpu.VMEM((rows, HD), F32),
                pltpu.SemaphoreType.DMA((slots + 1,)),
                pltpu.SemaphoreType.DMA((1,)),
            ],
        ),
        compiler_params=pltpu.CompilerParams(vmem_limit_bytes=40 << 20),
        cost_estimate=pl.CostEstimate(
            flops=4 * rows * keys * HD + 2 * BLK * width * cols,
            bytes_accessed=2 * (keys * 2 * HD + w_out.size + BLK * (width + cols)),
            transcendentals=rows * keys,
        ),
    )(meta, anc, q, kv, w_out)


def norm_kernel(res_ref, own_ref, u1_ref, u2_ref, v1_ref, v2_ref, gain_ref, keep_ref, o_ref):
    half = u1_ref.shape[1]
    total = []
    for lo, u, v in ((0, u1_ref, v1_ref), (half, u2_ref, v2_ref)):
        total.append(
            res_ref[:, lo:lo + half].astype(F32)
            + own_ref[:, lo:lo + half].astype(F32)
            + u[...].astype(F32)
            + v[...].astype(F32)
        )
    square = sum(jnp.sum(x * x, axis=1, keepdims=True) for x in total)
    factor = lax.rsqrt(square * (1.0 / (2 * half)) + 1e-06) * keep_ref[0].astype(F32)
    for lo, x in zip((0, half), total):
        o_ref[:, lo:lo + half] = (x * factor * gain_ref[:, lo:lo + half]).astype(BF16)


def final_norm(residual, own, u, v, gain, keep):
    rows, cols = residual.shape
    vm = pl.BlockSpec(memory_space=pltpu.VMEM)
    return pl.pallas_call(
        norm_kernel,
        name="final_norm",
        out_shape=jax.ShapeDtypeStruct((rows, cols), BF16),
        in_specs=[vm] * 7 + [pl.BlockSpec(memory_space=pltpu.SMEM)],
        out_specs=vm,
        compiler_params=pltpu.CompilerParams(vmem_limit_bytes=30 << 20),
    )(residual, own, *u, *v, gain[None, :], keep)


def ring(n, s):
    return [(i, (i + s) % n) for i in range(n)]


def on_device(activations, residual, w_query, w_key, w_value, w_out, gain, ancestors, kept):
    blk_dev = ancestors.shape[0]
    kv_own = kv_project(activations, w_key, w_value)
    kv = lax.all_gather(kv_own, CTX, axis=0, tiled=True)
    queries = jnp.dot(activations, w_query, preferred_element_type=F32).astype(BF16)

    t = lax.axis_index("tp").astype(jnp.int32)
    position = lax.axis_index(CTX).astype(jnp.int32)

    def term(s):
        local = (t + s) % 4
        meta = jnp.stack([local, position * blk_dev + local])
        return block_term(meta, ancestors, queries, kv, w_out)

    def send(x, s):
        return lax.ppermute(x, "tp", ring(4, s))

    half = w_out.shape[1] // 2
    p2 = term(2)
    a = send(p2[:, :half], 1)
    b = send(p2[:, half:], 3)
    p1 = term(1)
    u2 = send(p1[:, half:], 1)
    p3 = term(3)
    v1 = send(p3[:, :half], 3)
    p0 = term(0)
    u1 = send(p1[:, :half] + a, 1)
    v2 = send(p3[:, half:] + b, 3)
    keep = lax.dynamic_slice_in_dim(kept, t, 1, 0)
    return final_norm(residual, p0, (u1, u2), (v1, v2), gain, keep)


def solution(mesh):
    fine = Mesh(mesh.devices.reshape(2, 4, 2, 2, 4), ("dp", "z", "y", "core", "tp"))
    ctx = ("dp",) + CTX
    in_specs = (
        P(ctx, None),
        P(ctx + ("tp",), None),
        P(None, "tp"),
        P(None, "tp"),
        P(None, "tp"),
        P("tp", None),
        P(),
        P(ctx, None),
        P(ctx),
    )
    out_specs = P(ctx + ("tp",), None)
    return jax.shard_map(
        on_device, mesh=fine, in_specs=in_specs, out_specs=out_specs, check_vma=False
    )
```

```python
import math

import jax
import jax.numpy as jnp
from jax import lax
from jax.experimental import pallas as pl
from jax.experimental.pallas import tpu as pltpu
from jax.sharding import Mesh, PartitionSpec as P

HD = 128
BLK = 128
CHUNK = 4
CTX = ("z", "y", "core")
F32 = jnp.float32
BF16 = jnp.bfloat16
SCALE2 = math.log2(math.e) / math.sqrt(HD)
NT = (((1,), (1,)), ((), ()))


def kv_kernel(x_ref, wk_ref, wv_ref, o_ref, xbuf, wbuf, sems):
    parts, _, tile = xbuf.shape
    copies = []
    for k in range(parts):
        cut = pl.ds(k * tile, tile)
        group = [
            pltpu.make_async_copy(x_ref.at[:, cut], xbuf.at[k], sems.at[0, k]),
            pltpu.make_async_copy(wk_ref.at[cut], wbuf.at[k, :, pl.ds(0, HD)], sems.at[1, k]),
            pltpu.make_async_copy(wv_ref.at[cut], wbuf.at[k, :, pl.ds(HD, HD)], sems.at[2, k]),
        ]
        for copy in group:
            copy.start()
        copies.append(group)
    total = None
    for k in range(parts):
        for copy in copies[k]:
            copy.wait()
        part = jnp.dot(xbuf[k], wbuf[k], preferred_element_type=F32)
        total = part if total is None else total + part
    o_ref[...] = total.astype(BF16)


def kv_project(x, wk, wv):
    rows, depth = x.shape
    parts = 10
    tile = depth // parts
    hbm = pl.BlockSpec(memory_space=pltpu.HBM)
    return pl.pallas_call(
        kv_kernel,
        name="kv_project",
        out_shape=jax.ShapeDtypeStruct((rows, 2 * HD), BF16),
        in_specs=[hbm] * 3,
        out_specs=pl.BlockSpec(memory_space=pltpu.VMEM),
        scratch_shapes=[
            pltpu.VMEM((parts, rows, tile), BF16),
            pltpu.VMEM((parts, tile, 2 * HD), BF16),
            pltpu.SemaphoreType.DMA((3, parts)),
        ],
        cost_estimate=pl.CostEstimate(
            flops=2 * rows * depth * 2 * HD,
            bytes_accessed=2 * depth * (rows + 2 * HD),
            transcendentals=0,
        ),
    )(x, wk, wv)


def block_kernel(
    meta_ref, anc_ref, q_ref, kv_ref, w_ref, lo_ref, hi_ref,
    kvbuf, kvown, wbuf, sbuf, mbuf, lbuf, abuf, sems, wsem,
):
    local, own = meta_ref[0], meta_ref[1]
    slots = anc_ref.shape[1]
    heads = q_ref.shape[1] // HD
    wide = CHUNK * BLK

    own_copy = pltpu.make_async_copy(
        kv_ref.at[pl.ds(pl.multiple_of(own * BLK, BLK), BLK)], kvown, sems.at[slots]
    )
    own_copy.start()
    count = jnp.int32(0)
    for l in range(slots):
        entry = anc_ref[local, l]
        count += jnp.where(entry >= 0, 1, 0).astype(jnp.int32)
        src = pl.multiple_of(jnp.maximum(entry, 0) * BLK, BLK)
        pltpu.make_async_copy(
            kv_ref.at[pl.ds(src, BLK)], kvbuf.at[pl.ds(l * BLK, BLK)], sems.at[l]
        ).start()
    w_copy = pltpu.make_async_copy(w_ref, wbuf, wsem.at[0])
    w_copy.start()

    q_all = q_ref[...]
    q = jnp.concatenate([q_all[:, h * HD:(h + 1) * HD] for h in range(heads)], axis=0)
    own_copy.wait()
    s_own = lax.dot_general(q, kvown[:, :HD], NT, preferred_element_type=F32)
    row = lax.broadcasted_iota(jnp.int32, s_own.shape, 0) % BLK
    col = lax.broadcasted_iota(jnp.int32, s_own.shape, 1)
    s_own = jnp.where(col <= row, s_own, -jnp.inf)
    mbuf[...] = s_own
    for l in range(slots):
        pltpu.make_async_copy(
            kv_ref.at[pl.ds(0, BLK)], kvbuf.at[pl.ds(l * BLK, BLK)], sems.at[l]
        ).wait()
    chunks = (count + CHUNK - 1) // CHUNK

    def score(c, _):
        base = pl.multiple_of(c * wide, wide)
        s = lax.dot_general(q, kvbuf[pl.ds(base, wide), :HD], NT, preferred_element_type=F32)
        m = mbuf[...]
        for j in range(CHUNK):
            piece = s[:, j * BLK:(j + 1) * BLK]
            piece = jnp.where(c * CHUNK + j < count, piece, -jnp.inf)
            sbuf[c, :, j * BLK:(j + 1) * BLK] = piece
            m = jnp.maximum(m, piece)
        mbuf[...] = m
        return 0

    lax.fori_loop(0, chunks, score, 0)
    m = jnp.max(mbuf[...], axis=1, keepdims=True)
    p = jnp.exp2((s_own - m) * SCALE2)
    lbuf[...] = p
    abuf[...] = jnp.dot(p.astype(BF16), kvown[:, HD:], preferred_element_type=F32)

    def weigh(c, _):
        base = pl.multiple_of(c * wide, wide)
        w = jnp.exp2((sbuf[c] - m) * SCALE2)
        total = lbuf[...]
        for j in range(CHUNK):
            total += w[:, j * BLK:(j + 1) * BLK]
        lbuf[...] = total
        abuf[...] += jnp.dot(
            w.astype(BF16), kvbuf[pl.ds(base, wide), HD:], preferred_element_type=F32
        )
        return 0

    lax.fori_loop(0, chunks, weigh, 0)
    total = jnp.sum(lbuf[...], axis=1, keepdims=True)
    out = (abuf[...] / total).astype(BF16)
    head_out = jnp.concatenate([out[h * BLK:(h + 1) * BLK] for h in range(heads)], axis=1)
    w_copy.wait()
    half = lo_ref.shape[1]
    step = half // 2
    for o_ref, start in ((lo_ref, 0), (hi_ref, half)):
        for c in range(0, half, step):
            o_ref[:, c:c + step] = jnp.dot(
                head_out, wbuf[:, start + c:start + c + step], preferred_element_type=F32
            ).astype(BF16)


def block_term(meta, anc, q, kv, w_out):
    slots = anc.shape[1]
    width = q.shape[1]
    rows = BLK * (width // HD)
    cols = w_out.shape[1]
    keys = (slots + 1) * BLK
    return pl.pallas_call(
        block_kernel,
        name="block_term",
        out_shape=[jax.ShapeDtypeStruct((BLK, cols // 2), BF16)] * 2,
        grid_spec=pltpu.PrefetchScalarGridSpec(
            num_scalar_prefetch=2,
            grid=(1,),
            in_specs=[
                pl.BlockSpec((BLK, width), lambda i, meta, anc: (meta[0], 0)),
                pl.BlockSpec(memory_space=pltpu.HBM),
                pl.BlockSpec(memory_space=pltpu.HBM),
            ],
            out_specs=[pl.BlockSpec((BLK, cols // 2), lambda i, meta, anc: (0, 0))] * 2,
            scratch_shapes=[
                pltpu.VMEM((slots * BLK, 2 * HD), BF16),
                pltpu.VMEM((BLK, 2 * HD), BF16),
                pltpu.VMEM(w_out.shape, BF16),
                pltpu.VMEM((slots // CHUNK, rows, CHUNK * BLK), F32),
                pltpu.VMEM((rows, BLK), F32),
                pltpu.VMEM((rows, BLK), F32),
                pltpu.VMEM((rows, HD), F32),
                pltpu.SemaphoreType.DMA((slots + 1,)),
                pltpu.SemaphoreType.DMA((1,)),
            ],
        ),
        cost_estimate=pl.CostEstimate(flops=1 << 20, bytes_accessed=1 << 20, transcendentals=0),
    )(meta, anc, q, kv, w_out)


def norm_kernel(res_ref, o1_ref, o2_ref, u1_ref, u2_ref, v1_ref, v2_ref, gain_ref, keep_ref, o_ref):
    half = u1_ref.shape[1]
    total = []
    for lo, o, u, v in ((0, o1_ref, u1_ref, v1_ref), (half, o2_ref, u2_ref, v2_ref)):
        total.append(
            res_ref[:, lo:lo + half].astype(F32)
            + o[...].astype(F32)
            + u[...].astype(F32)
            + v[...].astype(F32)
        )
    square = sum(jnp.sum(x * x, axis=1, keepdims=True) for x in total)
    factor = lax.rsqrt(square * (1.0 / (2 * half)) + 1e-06) * keep_ref[0].astype(F32)
    for lo, x in zip((0, half), total):
        o_ref[:, lo:lo + half] = (x * factor * gain_ref[:, lo:lo + half]).astype(BF16)


def final_norm(residual, own, u, v, gain, keep):
    rows, cols = residual.shape
    vm = pl.BlockSpec(memory_space=pltpu.VMEM)
    return pl.pallas_call(
        norm_kernel,
        name="final_norm",
        out_shape=jax.ShapeDtypeStruct((rows, cols), BF16),
        in_specs=[vm] * 8 + [pl.BlockSpec(memory_space=pltpu.SMEM)],
        out_specs=vm,
        compiler_params=pltpu.CompilerParams(vmem_limit_bytes=30 << 20),
    )(residual, *own, *u, *v, gain[None, :], keep)


def ring(n, s):
    return [(i, (i + s) % n) for i in range(n)]


def on_device(activations, residual, w_query, w_key, w_value, w_out, gain, ancestors, kept):
    blk_dev = ancestors.shape[0]
    kv_own = kv_project(activations, w_key, w_value)
    kv = lax.all_gather(kv_own, CTX, axis=0, tiled=True)
    queries = jnp.dot(activations, w_query, preferred_element_type=F32).astype(BF16)

    t = lax.axis_index("tp").astype(jnp.int32)
    position = lax.axis_index(CTX).astype(jnp.int32)

    def term(s):
        local = (t + s) % 4
        meta = jnp.stack([local, position * blk_dev + local])
        return block_term(meta, ancestors, queries, kv, w_out)

    def send(x, s):
        return lax.ppermute(x, "tp", ring(4, s))

    lo2, hi2 = term(2)
    a = send(lo2, 1)
    b = send(hi2, 3)
    lo1, hi1 = term(1)
    u2 = send(hi1, 1)
    lo3, hi3 = term(3)
    v1 = send(lo3, 3)
    own = term(0)
    u1 = send(lo1 + a, 1)
    v2 = send(hi3 + b, 3)
    keep = lax.dynamic_slice_in_dim(kept, t, 1, 0)
    return final_norm(residual, own, (u1, u2), (v1, v2), gain, keep)


def solution(mesh):
    fine = Mesh(mesh.devices.reshape(2, 4, 2, 2, 4), ("dp", "z", "y", "core", "tp"))
    ctx = ("dp",) + CTX
    in_specs = (
        P(ctx, None),
        P(ctx + ("tp",), None),
        P(None, "tp"),
        P(None, "tp"),
        P(None, "tp"),
        P("tp", None),
        P(),
        P(ctx, None),
        P(ctx),
    )
    out_specs = P(ctx + ("tp",), None)
    return jax.shard_map(
        on_device, mesh=fine, in_specs=in_specs, out_specs=out_specs, check_vma=False
    )
```

```python
import functools
import math

import jax
import jax.numpy as jnp
from jax import lax
from jax.experimental import pallas as pl
from jax.experimental.pallas import tpu as pltpu
from jax.sharding import Mesh, PartitionSpec as P

HD = 128
BLK = 128
CHUNK = 4
CTX = ("z", "y", "core")
F32 = jnp.float32
BF16 = jnp.bfloat16
SCALE2 = math.log2(math.e) / math.sqrt(HD)
SPLIT = ((0, 3), (3, 5))
KERNEL_VMEM = 54 << 20
NT = (((1,), (1,)), ((), ()))


def kv_kernel(x_ref, wk_ref, wv_ref, o_ref, xbuf, wbuf, sems):
    parts, _, tile = xbuf.shape
    copies = []
    for k in range(parts):
        cut = pl.ds(k * tile, tile)
        group = [
            pltpu.make_async_copy(x_ref.at[:, cut], xbuf.at[k], sems.at[0, k]),
            pltpu.make_async_copy(wk_ref.at[cut], wbuf.at[k, :, pl.ds(0, HD)], sems.at[1, k]),
            pltpu.make_async_copy(wv_ref.at[cut], wbuf.at[k, :, pl.ds(HD, HD)], sems.at[2, k]),
        ]
        for copy in group:
            copy.start()
        copies.append(group)
    total = None
    for k in range(parts):
        for copy in copies[k]:
            copy.wait()
        part = jnp.dot(xbuf[k], wbuf[k], preferred_element_type=F32)
        total = part if total is None else total + part
    o_ref[...] = total.astype(BF16)


def kv_project(x, wk, wv):
    rows, depth = x.shape
    parts = 10
    tile = depth // parts
    hbm = pl.BlockSpec(memory_space=pltpu.HBM)
    return pl.pallas_call(
        kv_kernel,
        name="kv_project",
        out_shape=jax.ShapeDtypeStruct((rows, 2 * HD), BF16),
        in_specs=[hbm] * 3,
        out_specs=pl.BlockSpec(memory_space=pltpu.VMEM),
        scratch_shapes=[
            pltpu.VMEM((parts, rows, tile), BF16),
            pltpu.VMEM((parts, tile, 2 * HD), BF16),
            pltpu.SemaphoreType.DMA((3, parts)),
        ],
        cost_estimate=pl.CostEstimate(
            flops=2 * rows * depth * 2 * HD,
            bytes_accessed=2 * depth * (rows + 2 * HD),
            transcendentals=0,
        ),
    )(x, wk, wv)


def attend(q, kv_ref, own_row, rows, count):
    slots = len(rows)
    take = [kv_ref[pl.ds(pl.multiple_of(r, BLK), BLK), :] for r in rows]
    own = kv_ref[pl.ds(pl.multiple_of(own_row, BLK), BLK), :]
    groups = [take[c:c + CHUNK] for c in range(0, slots, CHUNK)]
    keys = [jnp.concatenate([x[:, :HD] for x in g], axis=0) for g in groups]
    values = [jnp.concatenate([x[:, HD:] for x in g], axis=0) for g in groups]
    results = []
    for lo, hi in SPLIT:
        part = q[lo * BLK:hi * BLK]
        s = lax.dot_general(part, own[:, :HD], NT, preferred_element_type=F32)
        row = lax.broadcasted_iota(jnp.int32, s.shape, 0) % BLK
        col = lax.broadcasted_iota(jnp.int32, s.shape, 1)
        pieces = [jnp.where(col <= row, s, -jnp.inf)]
        for c, key in enumerate(keys):
            s = lax.dot_general(part, key, NT, preferred_element_type=F32)
            for j in range(CHUNK):
                pieces.append(
                    jnp.where(c * CHUNK + j < count, s[:, j * BLK:(j + 1) * BLK], -jnp.inf)
                )
        top = pieces[0]
        for piece in pieces[1:]:
            top = jnp.maximum(top, piece)
        top = jnp.max(top, axis=1, keepdims=True)
        weights = [jnp.exp2((piece - top) * SCALE2) for piece in pieces]
        total = weights[0]
        for w in weights[1:]:
            total = total + w
        out = jnp.dot(weights[0].astype(BF16), own[:, HD:], preferred_element_type=F32)
        for c, value in enumerate(values):
            w = jnp.concatenate(
                [x.astype(BF16) for x in weights[1 + c * CHUNK:1 + (c + 1) * CHUNK]], axis=1
            )
            out = out + jnp.dot(w, value, preferred_element_type=F32)
        out = (out / jnp.sum(total, axis=1, keepdims=True)).astype(BF16)
        results += [out[h * BLK:(h + 1) * BLK] for h in range(hi - lo)]
    return jnp.concatenate(results, axis=1)


def block_kernel(places, order_ref, rows_ref, q_ref, w_ref, *rest):
    pieces, outs = rest[:len(places)], rest[len(places):-4]
    kvbuf, wbuf, sems, wsem = rest[-4:]
    step = pl.program_id(0)
    w_copy = pltpu.make_async_copy(w_ref, wbuf, wsem.at[0])

    copies = []
    for piece, spots in zip(pieces, places):
        size = piece.shape[0] // len(spots)
        for k, spot in enumerate(spots):
            copies.append(
                pltpu.make_async_copy(
                    piece.at[pl.ds(k * size, size)],
                    kvbuf.at[pl.ds(spot, size)],
                    sems.at[len(copies)],
                )
            )

    @pl.when(step == 0)
    def _():
        for copy in copies:
            copy.start()
        w_copy.start()
        for copy in copies:
            copy.wait()

    local = order_ref[step]
    slots = rows_ref.shape[1]
    rows, count = [], jnp.int32(0)
    for l in range(slots):
        entry = rows_ref[local, l]
        count += jnp.where(entry >= 0, 1, 0).astype(jnp.int32)
        rows.append(jnp.maximum(entry, 0))
    q_all = q_ref[...]
    heads = q_all.shape[1] // HD
    q = jnp.concatenate([q_all[:, h * HD:(h + 1) * HD] for h in range(heads)], axis=0)
    head_out = attend(q, kvbuf, local * BLK, rows, count)

    @pl.when(step == 0)
    def _():
        w_copy.wait()

    half = outs[0].shape[1]
    tile = half // 2
    for side in range(2):
        for c in range(0, half, tile):
            start = side * half + c
            part = jnp.dot(
                head_out, wbuf[:, start:start + tile], preferred_element_type=F32
            ).astype(BF16)
            for k in range(len(outs) // 2):
                @pl.when(step == k)
                def _():
                    outs[2 * k + side][:, c:c + tile] = part


def block_terms(order, rows, q, kv, w_out):
    pieces, places = zip(*kv)
    keys = sum(x.shape[0] for x in pieces)
    moves = sum(len(x) for x in places)
    count = order.shape[0]
    width = q.shape[1]
    cols = w_out.shape[1]
    outs = pl.pallas_call(
        functools.partial(block_kernel, places),
        name="block_terms",
        out_shape=[jax.ShapeDtypeStruct((BLK, cols // 2), BF16)] * (2 * count),
        grid_spec=pltpu.PrefetchScalarGridSpec(
            num_scalar_prefetch=2,
            grid=(count,),
            in_specs=[
                pl.BlockSpec((BLK, width), lambda i, order, rows: (order[i], 0)),
                pl.BlockSpec(memory_space=pltpu.HBM),
            ]
            + [pl.BlockSpec(memory_space=pl.ANY)] * len(pieces),
            out_specs=[pl.BlockSpec((BLK, cols // 2), lambda i, order, rows: (0, 0))]
            * (2 * count),
            scratch_shapes=[
                pltpu.VMEM((keys, 2 * HD), BF16),
                pltpu.VMEM(w_out.shape, BF16),
                pltpu.SemaphoreType.DMA((moves,)),
                pltpu.SemaphoreType.DMA((1,)),
            ],
        ),
        compiler_params=pltpu.CompilerParams(vmem_limit_bytes=KERNEL_VMEM),
        cost_estimate=pl.CostEstimate(flops=1 << 20, bytes_accessed=1 << 20, transcendentals=0),
    )(order, rows, q, w_out, *pieces)
    return [(outs[2 * k], outs[2 * k + 1]) for k in range(count)]


def norm_kernel(res_ref, o1_ref, o2_ref, u1_ref, u2_ref, v1_ref, v2_ref, gain_ref, keep_ref, o_ref):
    half = u1_ref.shape[1]
    total = []
    for lo, o, u, v in ((0, o1_ref, u1_ref, v1_ref), (half, o2_ref, u2_ref, v2_ref)):
        total.append(
            res_ref[:, lo:lo + half].astype(F32)
            + o[...].astype(F32)
            + u[...].astype(F32)
            + v[...].astype(F32)
        )
    square = sum(jnp.sum(x * x, axis=1, keepdims=True) for x in total)
    factor = lax.rsqrt(square * (1.0 / (2 * half)) + 1e-06) * keep_ref[0].astype(F32)
    for lo, x in zip((0, half), total):
        o_ref[:, lo:lo + half] = (x * factor * gain_ref[:, lo:lo + half]).astype(BF16)


def final_norm(residual, own, u, v, gain, keep):
    rows, cols = residual.shape
    vm = pl.BlockSpec(memory_space=pltpu.VMEM)
    return pl.pallas_call(
        norm_kernel,
        name="final_norm",
        out_shape=jax.ShapeDtypeStruct((rows, cols), BF16),
        in_specs=[vm] * 8 + [pl.BlockSpec(memory_space=pltpu.SMEM)],
        out_specs=vm,
        compiler_params=pltpu.CompilerParams(vmem_limit_bytes=30 << 20),
    )(residual, *own, *u, *v, gain[None, :], keep)


def ring(n, s):
    return [(i, (i + s) % n) for i in range(n)]


def shift(x, axis, s):
    return lax.ppermute(x, axis, ring({"y": 2, "core": 2, "z": 4, "tp": 4}[axis], s))


def gather_blocks(own, queries_of):
    rows = own.shape[0]
    half = rows // 2
    own_c = shift(own, "core", 1)
    y = shift(own, "y", 1)
    up = shift(own, "z", 3)
    down = shift(own, "z", 1)
    queries, y, up, down = lax.optimization_barrier((queries_of(), y, up, down))
    y_up = shift(y, "z", 3)
    y_down = shift(y, "z", 1)
    far_a = shift(up[:half], "z", 3)
    far_b = shift(down[half:], "z", 1)
    y_far = shift(y, "z", 2)
    first = shift(jnp.concatenate([y, up, down], axis=0), "core", 1)
    second = shift(jnp.concatenate([y_up, y_down, far_a, far_b, y_far], axis=0), "core", 1)
    spot = lambda dz, dy, dc: (dz * 4 + dy * 2 + dc) * rows
    return queries, [
        (own, (spot(0, 0, 0),)),
        (own_c, (spot(0, 0, 1),)),
        (y, (spot(0, 1, 0),)),
        (up, (spot(1, 0, 0),)),
        (down, (spot(3, 0, 0),)),
        (first, (spot(0, 1, 1), spot(1, 0, 1), spot(3, 0, 1))),
        (y_up, (spot(1, 1, 0),)),
        (y_down, (spot(3, 1, 0),)),
        (far_a, (spot(2, 0, 0),)),
        (far_b, (spot(2, 0, 0) + half,)),
        (y_far, (spot(2, 1, 0),)),
        (second, (spot(1, 1, 1), spot(3, 1, 1), spot(2, 0, 1), spot(2, 1, 1))),
    ]


def block_rows(ancestors):
    per = ancestors.shape[0]
    owner = ancestors // per
    dz = (owner // 4 - lax.axis_index("z")) % 4
    dy = (owner // 2 - lax.axis_index("y")) % 2
    dc = (owner - lax.axis_index("core")) % 2
    row = ((dz * 4 + dy * 2 + dc) * per + ancestors % per) * BLK
    return jnp.where(ancestors >= 0, row, -1).astype(jnp.int32)


def on_device(activations, residual, w_query, w_key, w_value, w_out, gain, ancestors, kept):
    kv_own = kv_project(activations, w_key, w_value)
    queries, kv = gather_blocks(
        kv_own,
        lambda: jnp.dot(activations, w_query, preferred_element_type=F32).astype(BF16),
    )
    rows = block_rows(ancestors)
    t = lax.axis_index("tp").astype(jnp.int32)
    order = (t + jnp.array([2, 1, 3, 0], jnp.int32)) % 4

    def send(x, s):
        return shift(x, "tp", s % 4)

    ((lo2, hi2),) = block_terms(order[:1], rows, queries, kv, w_out)
    a = send(lo2, 1)
    b = send(hi2, 3)
    (lo1, hi1), (lo3, hi3), own = block_terms(order[1:], rows, queries, kv, w_out)
    u2 = send(hi1, 1)
    v1 = send(lo3, 3)
    u1 = send(lo1 + a, 1)
    v2 = send(hi3 + b, 3)
    keep = lax.dynamic_slice_in_dim(kept, t, 1, 0)
    return final_norm(residual, own, (u1, u2), (v1, v2), gain, keep)


def solution(mesh):
    fine = Mesh(mesh.devices.reshape(2, 4, 2, 2, 4), ("dp", "z", "y", "core", "tp"))
    ctx = ("dp",) + CTX
    in_specs = (
        P(ctx, None),
        P(ctx + ("tp",), None),
        P(None, "tp"),
        P(None, "tp"),
        P(None, "tp"),
        P("tp", None),
        P(),
        P(ctx, None),
        P(ctx),
    )
    out_specs = P(ctx + ("tp",), None)
    return jax.shard_map(
        on_device, mesh=fine, in_specs=in_specs, out_specs=out_specs, check_vma=False
    )
```

```python
import functools
import math

import jax
import jax.numpy as jnp
from jax import lax
from jax.experimental import pallas as pl
from jax.experimental.pallas import tpu as pltpu
from jax.sharding import Mesh, PartitionSpec as P

HD = 128
BLK = 128
CHUNK = 4
CTX = ("z", "y", "core")
F32 = jnp.float32
BF16 = jnp.bfloat16
SCALE2 = math.log2(math.e) / math.sqrt(HD)
SPLIT = ((0, 3), (3, 5))
KERNEL_VMEM = 54 << 20
NT = (((1,), (1,)), ((), ()))


def kv_kernel(x_ref, wk_ref, wv_ref, o_ref, xbuf, wbuf, sems):
    parts, _, tile = xbuf.shape
    copies = []
    for k in range(parts):
        cut = pl.ds(k * tile, tile)
        group = [
            pltpu.make_async_copy(x_ref.at[:, cut], xbuf.at[k], sems.at[0, k]),
            pltpu.make_async_copy(wk_ref.at[cut], wbuf.at[k, :, pl.ds(0, HD)], sems.at[1, k]),
            pltpu.make_async_copy(wv_ref.at[cut], wbuf.at[k, :, pl.ds(HD, HD)], sems.at[2, k]),
        ]
        for copy in group:
            copy.start()
        copies.append(group)
    total = None
    for k in range(parts):
        for copy in copies[k]:
            copy.wait()
        part = jnp.dot(xbuf[k], wbuf[k], preferred_element_type=F32)
        total = part if total is None else total + part
    o_ref[...] = total.astype(BF16)


def kv_project(x, wk, wv):
    rows, depth = x.shape
    parts = 10
    tile = depth // parts
    hbm = pl.BlockSpec(memory_space=pltpu.HBM)
    return pl.pallas_call(
        kv_kernel,
        name="kv_project",
        out_shape=jax.ShapeDtypeStruct((rows, 2 * HD), BF16),
        in_specs=[hbm] * 3,
        out_specs=pl.BlockSpec(memory_space=pltpu.VMEM),
        scratch_shapes=[
            pltpu.VMEM((parts, rows, tile), BF16),
            pltpu.VMEM((parts, tile, 2 * HD), BF16),
            pltpu.SemaphoreType.DMA((3, parts)),
        ],
        cost_estimate=pl.CostEstimate(
            flops=2 * rows * depth * 2 * HD,
            bytes_accessed=2 * depth * (rows + 2 * HD),
            transcendentals=0,
        ),
    )(x, wk, wv)


def attend(q, kv_ref, own_row, rows, count):
    slots = len(rows)
    take = [kv_ref[pl.ds(pl.multiple_of(r, BLK), BLK), :] for r in rows]
    own = kv_ref[pl.ds(pl.multiple_of(own_row, BLK), BLK), :]
    groups = [take[c:c + CHUNK] for c in range(0, slots, CHUNK)]
    keys = [jnp.concatenate([x[:, :HD] for x in g], axis=0) for g in groups]
    values = [jnp.concatenate([x[:, HD:] for x in g], axis=0) for g in groups]
    results = []
    for lo, hi in SPLIT:
        part = q[lo * BLK:hi * BLK]
        s = lax.dot_general(part, own[:, :HD], NT, preferred_element_type=F32)
        row = lax.broadcasted_iota(jnp.int32, s.shape, 0) % BLK
        col = lax.broadcasted_iota(jnp.int32, s.shape, 1)
        pieces = [jnp.where(col <= row, s, -jnp.inf)]
        for c, key in enumerate(keys):
            s = lax.dot_general(part, key, NT, preferred_element_type=F32)
            for j in range(CHUNK):
                pieces.append(
                    jnp.where(c * CHUNK + j < count, s[:, j * BLK:(j + 1) * BLK], -jnp.inf)
                )
        top = pieces[0]
        for piece in pieces[1:]:
            top = jnp.maximum(top, piece)
        top = jnp.max(top, axis=1, keepdims=True)
        weights = [jnp.exp2((piece - top) * SCALE2) for piece in pieces]
        total = weights[0]
        for w in weights[1:]:
            total = total + w
        out = jnp.dot(weights[0].astype(BF16), own[:, HD:], preferred_element_type=F32)
        for c, value in enumerate(values):
            w = jnp.concatenate(
                [x.astype(BF16) for x in weights[1 + c * CHUNK:1 + (c + 1) * CHUNK]], axis=1
            )
            out = out + jnp.dot(w, value, preferred_element_type=F32)
        out = (out / jnp.sum(total, axis=1, keepdims=True)).astype(BF16)
        results += [out[h * BLK:(h + 1) * BLK] for h in range(hi - lo)]
    return jnp.concatenate(results, axis=1)


def block_kernel(places, order_ref, rows_ref, q_ref, w_ref, *rest):
    pieces, outs = rest[:len(places)], rest[len(places):-4]
    kvbuf, wbuf, sems, wsem = rest[-4:]
    step = pl.program_id(0)
    w_copy = pltpu.make_async_copy(w_ref, wbuf, wsem.at[0])

    copies = []
    for piece, spots in zip(pieces, places):
        size = piece.shape[0] // len(spots)
        for k, spot in enumerate(spots):
            copies.append(
                pltpu.make_async_copy(
                    piece.at[pl.ds(k * size, size)],
                    kvbuf.at[pl.ds(spot, size)],
                    sems.at[len(copies)],
                )
            )

    @pl.when(step == 0)
    def _():
        for copy in copies:
            copy.start()
        w_copy.start()
        for copy in copies:
            copy.wait()

    local = order_ref[step]
    slots = rows_ref.shape[1]
    rows, count = [], jnp.int32(0)
    for l in range(slots):
        entry = rows_ref[local, l]
        count += jnp.where(entry >= 0, 1, 0).astype(jnp.int32)
        rows.append(jnp.maximum(entry, 0))
    q_all = q_ref[...]
    heads = q_all.shape[1] // HD
    q = jnp.concatenate([q_all[:, h * HD:(h + 1) * HD] for h in range(heads)], axis=0)
    head_out = attend(q, kvbuf, local * BLK, rows, count)

    @pl.when(step == 0)
    def _():
        w_copy.wait()

    half = outs[0].shape[1]
    tile = half // 2
    for side in range(2):
        for c in range(0, half, tile):
            start = side * half + c
            part = jnp.dot(
                head_out, wbuf[:, start:start + tile], preferred_element_type=F32
            ).astype(BF16)
            for k in range(len(outs) // 2):
                @pl.when(step == k)
                def _():
                    outs[2 * k + side][:, c:c + tile] = part


def block_terms(order, rows, q, kv, w_out):
    pieces, places = zip(*kv)
    keys = sum(x.shape[0] for x in pieces)
    moves = sum(len(x) for x in places)
    count = order.shape[0]
    width = q.shape[1]
    cols = w_out.shape[1]
    outs = pl.pallas_call(
        functools.partial(block_kernel, places),
        name="block_terms",
        out_shape=[jax.ShapeDtypeStruct((BLK, cols // 2), BF16)] * (2 * count),
        grid_spec=pltpu.PrefetchScalarGridSpec(
            num_scalar_prefetch=2,
            grid=(count,),
            in_specs=[
                pl.BlockSpec((BLK, width), lambda i, order, rows: (order[i], 0)),
                pl.BlockSpec(memory_space=pltpu.HBM),
            ]
            + [pl.BlockSpec(memory_space=pl.ANY)] * len(pieces),
            out_specs=[pl.BlockSpec((BLK, cols // 2), lambda i, order, rows: (0, 0))]
            * (2 * count),
            scratch_shapes=[
                pltpu.VMEM((keys, 2 * HD), BF16),
                pltpu.VMEM(w_out.shape, BF16),
                pltpu.SemaphoreType.DMA((moves,)),
                pltpu.SemaphoreType.DMA((1,)),
            ],
        ),
        compiler_params=pltpu.CompilerParams(vmem_limit_bytes=KERNEL_VMEM),
        cost_estimate=pl.CostEstimate(flops=1 << 20, bytes_accessed=1 << 20, transcendentals=0),
    )(order, rows, q, w_out, *pieces)
    return [(outs[2 * k], outs[2 * k + 1]) for k in range(count)]


def norm_kernel(res_ref, o1_ref, o2_ref, u1_ref, u2_ref, v1_ref, v2_ref, gain_ref, keep_ref, o_ref):
    half = u1_ref.shape[1]
    total = []
    for lo, o, u, v in ((0, o1_ref, u1_ref, v1_ref), (half, o2_ref, u2_ref, v2_ref)):
        total.append(
            res_ref[:, lo:lo + half].astype(F32)
            + o[...].astype(F32)
            + u[...].astype(F32)
            + v[...].astype(F32)
        )
    square = sum(jnp.sum(x * x, axis=1, keepdims=True) for x in total)
    factor = lax.rsqrt(square * (1.0 / (2 * half)) + 1e-06) * keep_ref[0].astype(F32)
    for lo, x in zip((0, half), total):
        o_ref[:, lo:lo + half] = (x * factor * gain_ref[:, lo:lo + half]).astype(BF16)


def final_norm(residual, own, u, v, gain, keep):
    rows, cols = residual.shape
    vm = pl.BlockSpec(memory_space=pltpu.VMEM)
    return pl.pallas_call(
        norm_kernel,
        name="final_norm",
        out_shape=jax.ShapeDtypeStruct((rows, cols), BF16),
        in_specs=[vm] * 8 + [pl.BlockSpec(memory_space=pltpu.SMEM)],
        out_specs=vm,
        compiler_params=pltpu.CompilerParams(vmem_limit_bytes=30 << 20),
    )(residual, *own, *u, *v, gain[None, :], keep)


def ring(n, s):
    return [(i, (i + s) % n) for i in range(n)]


def shift(x, axis, s):
    return lax.ppermute(x, axis, ring({"y": 2, "core": 2, "z": 4, "tp": 4}[axis], s))


def gather_blocks(own, queries_of):
    rows = own.shape[0]

    def fetch(dz, dy):
        pairs = [(i, ((i // 2 - dz) % 4) * 2 + (i + dy) % 2) for i in range(8)]
        return lax.ppermute(own, ("z", "y"), pairs)

    places = ((2, 1), (2, 0), (1, 1), (3, 1), (0, 1), (1, 0), (3, 0))
    early = [fetch(*p) for p in places[:5]]
    queries = queries_of()
    pieces = early + [fetch(*p) for p in places[5:]]
    result = []
    for (dz, dy), piece in zip(((0, 0),) + places, [own] + pieces):
        other = shift(piece, "core", 1)
        for dc, x in ((0, piece), (1, other)):
            result.append((x, ((dz * 4 + dy * 2 + dc) * rows,)))
    return queries, result


def block_rows(ancestors):
    per = ancestors.shape[0]
    owner = ancestors // per
    dz = (owner // 4 - lax.axis_index("z")) % 4
    dy = (owner // 2 - lax.axis_index("y")) % 2
    dc = (owner - lax.axis_index("core")) % 2
    row = ((dz * 4 + dy * 2 + dc) * per + ancestors % per) * BLK
    return jnp.where(ancestors >= 0, row, -1).astype(jnp.int32)


def on_device(activations, residual, w_query, w_key, w_value, w_out, gain, ancestors, kept):
    kv_own = kv_project(activations, w_key, w_value)
    queries, kv = gather_blocks(
        kv_own,
        lambda: jnp.dot(activations, w_query, preferred_element_type=F32).astype(BF16),
    )
    rows = block_rows(ancestors)
    t = lax.axis_index("tp").astype(jnp.int32)
    order = (t + jnp.array([2, 1, 3, 0], jnp.int32)) % 4

    def send(x, s):
        return shift(x, "tp", s % 4)

    ((lo2, hi2),) = block_terms(order[:1], rows, queries, kv, w_out)
    a = send(lo2, 1)
    b = send(hi2, 3)
    (lo1, hi1), (lo3, hi3) = block_terms(order[1:3], rows, queries, kv, w_out)
    u2 = send(hi1, 1)
    v1 = send(lo3, 3)
    (own,) = block_terms(order[3:], rows, queries, kv, w_out)
    u1 = send(lo1 + a, 1)
    v2 = send(hi3 + b, 3)
    keep = lax.dynamic_slice_in_dim(kept, t, 1, 0)
    return final_norm(residual, own, (u1, u2), (v1, v2), gain, keep)


def solution(mesh):
    fine = Mesh(mesh.devices.reshape(2, 4, 2, 2, 4), ("dp", "z", "y", "core", "tp"))
    ctx = ("dp",) + CTX
    in_specs = (
        P(ctx, None),
        P(ctx + ("tp",), None),
        P(None, "tp"),
        P(None, "tp"),
        P(None, "tp"),
        P("tp", None),
        P(),
        P(ctx, None),
        P(ctx),
    )
    out_specs = P(ctx + ("tp",), None)
    return jax.shard_map(
        on_device, mesh=fine, in_specs=in_specs, out_specs=out_specs, check_vma=False
    )
```

```python
import functools
import math

import jax
import jax.numpy as jnp
from jax import lax
from jax.experimental import pallas as pl
from jax.experimental.pallas import tpu as pltpu
from jax.sharding import Mesh, PartitionSpec as P

HD = 128
BLK = 128
CHUNK = 4
CTX = ("z", "y", "core")
F32 = jnp.float32
BF16 = jnp.bfloat16
SCALE2 = math.log2(math.e) / math.sqrt(HD)
SPLIT = ((0, 3), (3, 5))
KERNEL_VMEM = 36 << 20
SMALL_COST = pl.CostEstimate(flops=1 << 20, bytes_accessed=1 << 20, transcendentals=0)
NT = (((1,), (1,)), ((), ()))


def kv_kernel(x_ref, wk_ref, wv_ref, o_ref, xbuf, wbuf, sems):
    parts, tile, _ = wbuf.shape
    copies = []
    for k in range(parts):
        cut = pl.ds(k * tile, tile)
        group = [
            pltpu.make_async_copy(x_ref.at[:, cut], xbuf.at[:, cut], sems.at[0, k]),
            pltpu.make_async_copy(wk_ref.at[cut], wbuf.at[k, :, pl.ds(0, HD)], sems.at[1, k]),
            pltpu.make_async_copy(wv_ref.at[cut], wbuf.at[k, :, pl.ds(HD, HD)], sems.at[2, k]),
        ]
        for copy in group:
            copy.start()
        copies.append(group)
    total = None
    for k in range(parts):
        for copy in copies[k]:
            copy.wait()
        part = jnp.dot(
            xbuf[:, k * tile:(k + 1) * tile], wbuf[k], preferred_element_type=F32
        )
        total = part if total is None else total + part
    o_ref[...] = total.astype(BF16)


def kv_project(x, wk, wv):
    rows, depth = x.shape
    parts = 10
    hbm = pl.BlockSpec(memory_space=pltpu.HBM)
    vmem = pl.BlockSpec(memory_space=pltpu.VMEM)
    return pl.pallas_call(
        kv_kernel,
        name="kv_project",
        out_shape=[
            jax.ShapeDtypeStruct((rows, 2 * HD), BF16),
            jax.ShapeDtypeStruct((rows, depth), BF16),
        ],
        in_specs=[hbm] * 3,
        out_specs=[vmem] * 2,
        scratch_shapes=[
            pltpu.VMEM((parts, depth // parts, 2 * HD), BF16),
            pltpu.SemaphoreType.DMA((3, parts)),
        ],
        compiler_params=pltpu.CompilerParams(vmem_limit_bytes=52 << 20),
        cost_estimate=SMALL_COST,
    )(x, wk, wv)


def q_kernel(x_ref, w_ref, o_ref, wbuf, sems):
    parts, tile, _ = wbuf.shape
    copies = [
        pltpu.make_async_copy(w_ref.at[pl.ds(k * tile, tile)], wbuf.at[k], sems.at[k])
        for k in range(parts)
    ]
    for copy in copies:
        copy.start()
    total = None
    for k in range(parts):
        copies[k].wait()
        part = jnp.dot(x_ref[:, k * tile:(k + 1) * tile], wbuf[k], preferred_element_type=F32)
        total = part if total is None else total + part
    o_ref[...] = total.astype(BF16)


def q_project(x, w):
    parts = 5
    vmem = pl.BlockSpec(memory_space=pltpu.VMEM)
    return pl.pallas_call(
        q_kernel,
        name="q_project",
        out_shape=jax.ShapeDtypeStruct((x.shape[0], w.shape[1]), BF16),
        in_specs=[vmem, pl.BlockSpec(memory_space=pltpu.HBM)],
        out_specs=vmem,
        scratch_shapes=[
            pltpu.VMEM((parts, w.shape[0] // parts, w.shape[1]), BF16),
            pltpu.SemaphoreType.DMA((parts,)),
        ],
        compiler_params=pltpu.CompilerParams(vmem_limit_bytes=40 << 20),
        cost_estimate=SMALL_COST,
    )(x, w)


def collect_kernel(places, based, *refs):
    pieces, out, sems = refs[based:-2], refs[-2], refs[-1]
    copies = [
        pltpu.make_async_copy(piece, out.at[pl.ds(spot, piece.shape[0])], sems.at[k])
        for k, (piece, spot) in enumerate(zip(pieces, places))
    ]
    for copy in copies:
        copy.start()
    for copy in copies:
        copy.wait()


def collect(parts, shape, base=None):
    pieces, places = zip(*parts)
    based = 0 if base is None else 1
    return pl.pallas_call(
        functools.partial(collect_kernel, places, based),
        name="collect",
        out_shape=jax.ShapeDtypeStruct(shape, BF16),
        in_specs=[pl.BlockSpec(memory_space=pl.ANY)] * (based + len(pieces)),
        out_specs=pl.BlockSpec(memory_space=pl.ANY),
        scratch_shapes=[pltpu.SemaphoreType.DMA((len(pieces),))],
        input_output_aliases={0: 0} if based else {},
        compiler_params=pltpu.CompilerParams(vmem_limit_bytes=8 << 20),
        cost_estimate=SMALL_COST,
    )(*([base] if based else []), *pieces)


def attend(q, kv_ref, own_row, rows, count):
    slots = len(rows)
    take = [kv_ref[pl.ds(pl.multiple_of(r, BLK), BLK), :] for r in rows]
    own = kv_ref[pl.ds(pl.multiple_of(own_row, BLK), BLK), :]
    groups = [take[c:c + CHUNK] for c in range(0, slots, CHUNK)]
    keys = [jnp.concatenate([x[:, :HD] for x in g], axis=0) for g in groups]
    values = [jnp.concatenate([x[:, HD:] for x in g], axis=0) for g in groups]
    results = []
    for lo, hi in SPLIT:
        part = q[lo * BLK:hi * BLK]
        s = lax.dot_general(part, own[:, :HD], NT, preferred_element_type=F32)
        row = lax.broadcasted_iota(jnp.int32, s.shape, 0) % BLK
        col = lax.broadcasted_iota(jnp.int32, s.shape, 1)
        pieces = [jnp.where(col <= row, s, -jnp.inf)]
        for c, key in enumerate(keys):
            s = lax.dot_general(part, key, NT, preferred_element_type=F32)
            for j in range(CHUNK):
                pieces.append(
                    jnp.where(c * CHUNK + j < count, s[:, j * BLK:(j + 1) * BLK], -jnp.inf)
                )
        top = pieces[0]
        for piece in pieces[1:]:
            top = jnp.maximum(top, piece)
        top = jnp.max(top, axis=1, keepdims=True)
        weights = [jnp.exp2((piece - top) * SCALE2) for piece in pieces]
        total = weights[0]
        for w in weights[1:]:
            total = total + w
        out = jnp.dot(weights[0].astype(BF16), own[:, HD:], preferred_element_type=F32)
        for c, value in enumerate(values):
            w = jnp.concatenate(
                [x.astype(BF16) for x in weights[1 + c * CHUNK:1 + (c + 1) * CHUNK]], axis=1
            )
            out = out + jnp.dot(w, value, preferred_element_type=F32)
        out = (out / jnp.sum(total, axis=1, keepdims=True)).astype(BF16)
        results += [out[h * BLK:(h + 1) * BLK] for h in range(hi - lo)]
    return jnp.concatenate(results, axis=1)


def block_kernel(order_ref, rows_ref, q_ref, kv_ref, w_ref, *rest):
    res_ref, outs = (rest[0], rest[1:]) if len(rest) % 2 else (None, rest)
    step = pl.program_id(0)
    local = order_ref[step]
    slots = rows_ref.shape[1]
    rows, count = [], jnp.int32(0)
    for l in range(slots):
        entry = rows_ref[local, l]
        count += jnp.where(entry >= 0, 1, 0).astype(jnp.int32)
        rows.append(jnp.maximum(entry, 0))
    q_all = q_ref[...]
    heads = q_all.shape[1] // HD
    q = jnp.concatenate([q_all[:, h * HD:(h + 1) * HD] for h in range(heads)], axis=0)
    head_out = attend(q, kv_ref, local * BLK, rows, count)
    half = outs[0].shape[1]
    tile = half // 2
    for side in range(2):
        for c in range(0, half, tile):
            cut = slice(side * half + c, side * half + c + tile)
            part = jnp.dot(head_out, w_ref[:, cut], preferred_element_type=F32).astype(BF16)
            if res_ref is not None:
                part = part.astype(F32) + res_ref[:, cut].astype(F32)
            for k in range(len(outs) // 2):
                @pl.when(step == k)
                def _():
                    outs[2 * k + side][:, c:c + tile] = part


def block_terms(order, rows, q, kv, w_out, residual=None):
    count = order.shape[0]
    width = q.shape[1]
    cols = w_out.shape[1]
    vmem = pl.BlockSpec(memory_space=pltpu.VMEM)
    extra = [] if residual is None else [residual]
    kind = BF16 if residual is None else F32
    outs = pl.pallas_call(
        block_kernel,
        name="block_terms",
        out_shape=[jax.ShapeDtypeStruct((BLK, cols // 2), kind)] * (2 * count),
        grid_spec=pltpu.PrefetchScalarGridSpec(
            num_scalar_prefetch=2,
            grid=(count,),
            in_specs=[pl.BlockSpec((BLK, width), lambda i, order, rows: (order[i], 0)), vmem, vmem]
            + [vmem] * len(extra),
            out_specs=[vmem] * (2 * count),
        ),
        compiler_params=pltpu.CompilerParams(vmem_limit_bytes=KERNEL_VMEM),
        cost_estimate=SMALL_COST,
    )(order, rows, q, kv, w_out, *extra)
    return [(outs[2 * k], outs[2 * k + 1]) for k in range(count)]


def norm_kernel(b1_ref, b2_ref, u1_ref, u2_ref, v1_ref, v2_ref, gain_ref, keep_ref, o_ref):
    half = u1_ref.shape[1]
    total = [
        b[...] + u[...].astype(F32) + v[...].astype(F32)
        for b, u, v in ((b1_ref, u1_ref, v1_ref), (b2_ref, u2_ref, v2_ref))
    ]
    square = sum(jnp.sum(x * x, axis=1, keepdims=True) for x in total)
    factor = lax.rsqrt(square * (1.0 / (2 * half)) + 1e-06) * keep_ref[0].astype(F32)
    for lo, x in zip((0, half), total):
        o_ref[:, lo:lo + half] = (x * factor * gain_ref[:, lo:lo + half]).astype(BF16)


def final_norm(base, u, v, gain, keep):
    rows, half = base[0].shape
    vm = pl.BlockSpec(memory_space=pltpu.VMEM)
    return pl.pallas_call(
        norm_kernel,
        name="final_norm",
        out_shape=jax.ShapeDtypeStruct((rows, 2 * half), BF16),
        in_specs=[vm] * 7 + [pl.BlockSpec(memory_space=pltpu.SMEM)],
        out_specs=vm,
        compiler_params=pltpu.CompilerParams(vmem_limit_bytes=30 << 20),
    )(*base, *u, *v, gain[None, :], keep)


def ring(n, s):
    return [(i, (i + s) % n) for i in range(n)]


def shift(x, axis, s):
    return lax.ppermute(x, axis, ring({"y": 2, "core": 2, "z": 4, "tp": 4}[axis], s))


def gather_blocks(own, beside):
    rows = own.shape[0]
    shape = (16 * rows, own.shape[1])

    def fetch(x, dz, dy):
        pairs = [(i, ((i // 2 - dz) % 4) * 2 + (i + dy) % 2) for i in range(8)]
        return lax.ppermute(x, ("z", "y"), pairs)

    def both(dz, dy, piece):
        spot = (dz * 4 + dy * 2) * rows
        return [(piece, spot), (shift(piece, "core", 1), spot + rows)]

    places = ((2, 1), (2, 0), (1, 1), (3, 1), (0, 1), (1, 0), (3, 0))
    pieces = [fetch(own, *p) for p in places[:5]]
    extra = beside()
    pieces, own, extra = lax.optimization_barrier((pieces, own, extra))
    late = [fetch(own, *p) for p in places[5:]]
    early = both(0, 0, own)
    for p, piece in zip(places[:5], pieces):
        early += both(*p, piece)
    base = collect(early, shape)
    last = []
    for p, piece in zip(places[5:], late):
        last += both(*p, piece)
    return collect(last, shape, base), extra


def block_rows(ancestors):
    per = ancestors.shape[0]
    owner = ancestors // per
    dz = (owner // 4 - lax.axis_index("z")) % 4
    dy = (owner // 2 - lax.axis_index("y")) % 2
    dc = (owner - lax.axis_index("core")) % 2
    row = ((dz * 4 + dy * 2 + dc) * per + ancestors % per) * BLK
    return jnp.where(ancestors >= 0, row, -1).astype(jnp.int32)


def on_device(activations, residual, w_query, w_key, w_value, w_out, gain, ancestors, kept):
    kv_own, held = kv_project(activations, w_key, w_value)
    kv, (queries, w_held) = gather_blocks(
        kv_own, lambda: (q_project(held, w_query), collect([(w_out, 0)], w_out.shape))
    )
    rows = block_rows(ancestors)
    t = lax.axis_index("tp").astype(jnp.int32)
    order = (t + jnp.array([2, 1, 3, 0], jnp.int32)) % 4

    def send(x, s):
        return shift(x, "tp", s % 4)

    ((lo2, hi2),) = block_terms(order[:1], rows, queries, kv, w_held)
    a = send(lo2, 1)
    b = send(hi2, 3)
    (lo1, hi1), (lo3, hi3) = block_terms(order[1:3], rows, queries, kv, w_held)
    u2 = send(hi1, 1)
    v1 = send(lo3, 3)
    (base,) = block_terms(order[3:], rows, queries, kv, w_held, residual)
    u1 = send(lo1 + a, 1)
    v2 = send(hi3 + b, 3)
    keep = lax.dynamic_slice_in_dim(kept, t, 1, 0)
    return final_norm(base, (u1, u2), (v1, v2), gain, keep)


def solution(mesh):
    fine = Mesh(mesh.devices.reshape(2, 4, 2, 2, 4), ("dp", "z", "y", "core", "tp"))
    ctx = ("dp",) + CTX
    in_specs = (
        P(ctx, None),
        P(ctx + ("tp",), None),
        P(None, "tp"),
        P(None, "tp"),
        P(None, "tp"),
        P("tp", None),
        P(),
        P(ctx, None),
        P(ctx),
    )
    out_specs = P(ctx + ("tp",), None)
    return jax.shard_map(
        on_device, mesh=fine, in_specs=in_specs, out_specs=out_specs, check_vma=False
    )
```

```python
import functools
import math

import jax
import jax.numpy as jnp
from jax import lax
from jax.experimental import pallas as pl
from jax.experimental.pallas import tpu as pltpu
from jax.sharding import Mesh, PartitionSpec as P

HD = 128
BLK = 128
CHUNK = 4
CTX = ("z", "y", "core")
F32 = jnp.float32
BF16 = jnp.bfloat16
SCALE2 = math.log2(math.e) / math.sqrt(HD)
SPLIT = ((0, 3), (3, 5))
KERNEL_VMEM = 58 << 20
BLOCK_VMEM = 30 << 20
SMALL_COST = pl.CostEstimate(flops=1 << 20, bytes_accessed=1 << 20, transcendentals=0)
NT = (((1,), (1,)), ((), ()))


def kv_kernel(x_ref, wk_ref, wv_ref, o_ref, xbuf, wbuf, sems):
    parts, tile, _ = wbuf.shape
    copies = []
    for k in range(parts):
        cut = pl.ds(k * tile, tile)
        group = [
            pltpu.make_async_copy(x_ref.at[:, cut], xbuf.at[:, cut], sems.at[0, k]),
            pltpu.make_async_copy(wk_ref.at[cut], wbuf.at[k, :, pl.ds(0, HD)], sems.at[1, k]),
            pltpu.make_async_copy(wv_ref.at[cut], wbuf.at[k, :, pl.ds(HD, HD)], sems.at[2, k]),
        ]
        for copy in group:
            copy.start()
        copies.append(group)
    total = None
    for k in range(parts):
        for copy in copies[k]:
            copy.wait()
        part = jnp.dot(
            xbuf[:, k * tile:(k + 1) * tile], wbuf[k], preferred_element_type=F32
        )
        total = part if total is None else total + part
    o_ref[...] = total.astype(BF16)


def kv_project(x, wk, wv):
    rows, depth = x.shape
    parts = 5
    hbm = pl.BlockSpec(memory_space=pltpu.HBM)
    return pl.pallas_call(
        kv_kernel,
        name="kv_project",
        out_shape=jax.ShapeDtypeStruct((rows, 2 * HD), BF16),
        in_specs=[hbm] * 3,
        out_specs=pl.BlockSpec(memory_space=pltpu.VMEM),
        scratch_shapes=[
            pltpu.VMEM((rows, depth), BF16),
            pltpu.VMEM((parts, depth // parts, 2 * HD), BF16),
            pltpu.SemaphoreType.DMA((3, parts)),
        ],
        compiler_params=pltpu.CompilerParams(vmem_limit_bytes=KERNEL_VMEM),
        cost_estimate=SMALL_COST,
    )(x, wk, wv)


def q_kernel(x_ref, w_ref, o_ref, wbuf, sems):
    parts, tile, _ = wbuf.shape
    copies = [
        pltpu.make_async_copy(w_ref.at[pl.ds(k * tile, tile)], wbuf.at[k], sems.at[k])
        for k in range(parts)
    ]
    for copy in copies:
        copy.start()
    total = None
    for k in range(parts):
        copies[k].wait()
        part = jnp.dot(x_ref[:, k * tile:(k + 1) * tile], wbuf[k], preferred_element_type=F32)
        total = part if total is None else total + part
    o_ref[...] = total.astype(BF16)


def q_project(x, w):
    parts = 5
    vmem = pl.BlockSpec(memory_space=pltpu.VMEM)
    return pl.pallas_call(
        q_kernel,
        name="q_project",
        out_shape=jax.ShapeDtypeStruct((x.shape[0], w.shape[1]), BF16),
        in_specs=[vmem, pl.BlockSpec(memory_space=pltpu.HBM)],
        out_specs=vmem,
        scratch_shapes=[
            pltpu.VMEM((parts, w.shape[0] // parts, w.shape[1]), BF16),
            pltpu.SemaphoreType.DMA((parts,)),
        ],
        compiler_params=pltpu.CompilerParams(vmem_limit_bytes=20 << 20),
        cost_estimate=SMALL_COST,
    )(x, w)


def tie(values):
    spec = pl.BlockSpec(memory_space=pl.ANY)
    return pl.pallas_call(
        lambda *refs: None,
        name="tie",
        out_shape=[jax.ShapeDtypeStruct(x.shape, x.dtype) for x in values],
        in_specs=[spec] * len(values),
        out_specs=[spec] * len(values),
        input_output_aliases={k: k for k in range(len(values))},
        compiler_params=pltpu.CompilerParams(vmem_limit_bytes=1 << 20),
        cost_estimate=SMALL_COST,
    )(*values)


def collect_kernel(moves, based, *refs):
    pieces, out, sems = refs[based:based + len(moves)], refs[-2], refs[-1]
    copies = []
    for piece, cuts in zip(pieces, moves):
        for source, target, size in cuts:
            copies.append(
                pltpu.make_async_copy(
                    piece.at[pl.ds(source, size)],
                    out.at[pl.ds(target, size)],
                    sems.at[len(copies)],
                )
            )
    for copy in copies:
        copy.start()
    for copy in copies:
        copy.wait()


def collect(parts, shape, base=None, after=()):
    pieces, moves = zip(*parts)
    based = 0 if base is None else 1
    return pl.pallas_call(
        functools.partial(collect_kernel, moves, based),
        name="collect",
        out_shape=jax.ShapeDtypeStruct(shape, BF16),
        in_specs=[pl.BlockSpec(memory_space=pl.ANY)] * (based + len(pieces) + len(after)),
        out_specs=pl.BlockSpec(memory_space=pl.ANY),
        scratch_shapes=[pltpu.SemaphoreType.DMA((sum(len(x) for x in moves),))],
        input_output_aliases={0: 0} if based else {},
        compiler_params=pltpu.CompilerParams(vmem_limit_bytes=2 << 20),
        cost_estimate=SMALL_COST,
    )(*([base] if based else []), *pieces, *after)


def attend(q, kv_ref, own_row, rows, count):
    slots = len(rows)
    take = [kv_ref[pl.ds(pl.multiple_of(r, BLK), BLK), :] for r in rows]
    own = kv_ref[pl.ds(pl.multiple_of(own_row, BLK), BLK), :]
    groups = [take[c:c + CHUNK] for c in range(0, slots, CHUNK)]
    keys = [jnp.concatenate([x[:, :HD] for x in g], axis=0) for g in groups]
    values = [jnp.concatenate([x[:, HD:] for x in g], axis=0) for g in groups]
    results = []
    for lo, hi in SPLIT:
        part = q[lo * BLK:hi * BLK]
        s = lax.dot_general(part, own[:, :HD], NT, preferred_element_type=F32)
        row = lax.broadcasted_iota(jnp.int32, s.shape, 0) % BLK
        col = lax.broadcasted_iota(jnp.int32, s.shape, 1)
        pieces = [jnp.where(col <= row, s, -jnp.inf)]
        for c, key in enumerate(keys):
            s = lax.dot_general(part, key, NT, preferred_element_type=F32)
            for j in range(CHUNK):
                pieces.append(
                    jnp.where(c * CHUNK + j < count, s[:, j * BLK:(j + 1) * BLK], -jnp.inf)
                )
        top = pieces[0]
        for piece in pieces[1:]:
            top = jnp.maximum(top, piece)
        top = jnp.max(top, axis=1, keepdims=True)
        weights = [jnp.exp2((piece - top) * SCALE2) for piece in pieces]
        total = weights[0]
        for w in weights[1:]:
            total = total + w
        out = jnp.dot(weights[0].astype(BF16), own[:, HD:], preferred_element_type=F32)
        for c, value in enumerate(values):
            w = jnp.concatenate(
                [x.astype(BF16) for x in weights[1 + c * CHUNK:1 + (c + 1) * CHUNK]], axis=1
            )
            out = out + jnp.dot(w, value, preferred_element_type=F32)
        out = (out / jnp.sum(total, axis=1, keepdims=True)).astype(BF16)
        results += [out[h * BLK:(h + 1) * BLK] for h in range(hi - lo)]
    return jnp.concatenate(results, axis=1)


def block_row(entry, per):
    owner = entry // per
    dz = (owner // 4 - lax.axis_index("z") + 4) % 4
    dy = (owner // 2 + lax.axis_index("y")) % 2
    dc = (owner + lax.axis_index("core")) % 2
    return ((dz * 4 + dy * 2 + dc) * per + entry % per) * BLK


def block_kernel(turn, anc_ref, q_ref, kv_ref, w_ref, *rest):
    res_ref, outs = (rest[0], rest[1:3]) if len(rest) % 2 else (None, rest[:2])
    per, slots = anc_ref.shape
    local = (lax.axis_index("tp") + turn) % per
    rows, count = [], jnp.int32(0)
    for l in range(slots):
        entry = anc_ref[local, l]
        count += jnp.where(entry >= 0, 1, 0).astype(jnp.int32)
        rows.append(block_row(jnp.maximum(entry, 0), per))
    q_all = q_ref[pl.ds(pl.multiple_of(local * BLK, BLK), BLK), :]
    heads = q_all.shape[1] // HD
    q = jnp.concatenate([q_all[:, h * HD:(h + 1) * HD] for h in range(heads)], axis=0)
    head_out = attend(q, kv_ref, local * BLK, rows, count)
    half = outs[0].shape[1]
    tile = half // 2
    for side in range(2):
        for c in range(0, half, tile):
            cut = slice(side * half + c, side * half + c + tile)
            part = jnp.dot(head_out, w_ref[:, cut], preferred_element_type=F32).astype(BF16)
            if res_ref is not None:
                part = part.astype(F32) + res_ref[:, cut].astype(F32)
            outs[side][:, c:c + tile] = part


def block_terms(turn, ancestors, q, kv, w_out, residual=None):
    cols = w_out.shape[1]
    vmem = pl.BlockSpec(memory_space=pltpu.VMEM)
    extra = [] if residual is None else [residual]
    kind = BF16 if residual is None else F32
    outs = pl.pallas_call(
        functools.partial(block_kernel, turn),
        name="block_terms",
        out_shape=[jax.ShapeDtypeStruct((BLK, cols // 2), kind)] * 2
        + [jax.ShapeDtypeStruct(x.shape, x.dtype) for x in (kv, w_out)],
        in_specs=[pl.BlockSpec(memory_space=pltpu.SMEM)] + [vmem] * (3 + len(extra)),
        out_specs=[vmem] * 2 + [pl.BlockSpec(memory_space=pl.ANY)] * 2,
        input_output_aliases={2: 2, 3: 3},
        compiler_params=pltpu.CompilerParams(vmem_limit_bytes=BLOCK_VMEM),
        cost_estimate=SMALL_COST,
    )(ancestors, q, kv, w_out, *extra)
    return outs[:2], outs[2:]


def norm_kernel(b1_ref, b2_ref, u_ref, v_ref, gain_ref, keep_ref, o_ref):
    half = u_ref.shape[1]
    total = [b1_ref[...] + u_ref[...].astype(F32), b2_ref[...] + v_ref[...].astype(F32)]
    square = sum(jnp.sum(x * x, axis=1, keepdims=True) for x in total)
    factor = lax.rsqrt(square * (1.0 / (2 * half)) + 1e-06) * keep_ref[lax.axis_index("tp")].astype(F32)
    for lo, x in zip((0, half), total):
        o_ref[:, lo:lo + half] = (x * factor * gain_ref[:, lo:lo + half]).astype(BF16)


def final_norm(base, last, gain, keep):
    rows, half = base[0].shape
    vm = pl.BlockSpec(memory_space=pltpu.VMEM)
    return pl.pallas_call(
        norm_kernel,
        name="final_norm",
        out_shape=jax.ShapeDtypeStruct((rows, 2 * half), BF16),
        in_specs=[vm] * 5 + [pl.BlockSpec(memory_space=pltpu.SMEM)],
        out_specs=vm,
        compiler_params=pltpu.CompilerParams(vmem_limit_bytes=30 << 20),
    )(*base, *last, gain[None, :], keep)


def ring(n, s):
    return [(i, (i + s) % n) for i in range(n)]


def shift(x, axis, s):
    return lax.ppermute(x, axis, ring({"y": 2, "core": 2, "z": 4, "tp": 4}[axis], s))


def gather_blocks(own, first, second):
    rows = own.shape[0]
    half = rows // 2

    def fetch(x, dz, dy):
        pairs = [(i, ((i // 2 - dz) % 4) * 2 + (i + dy) % 2) for i in range(8)]
        return lax.ppermute(x, ("z", "y"), pairs)

    def both(piece, *moves):
        result, source = ([], []), 0
        for dz, dy, skip, size in moves:
            spot = (dz * 4 + dy * 2) * rows + skip
            for core in range(2):
                result[core].append((source, spot + core * rows, size))
            source += size
        return [(piece, tuple(result[0])), (shift(piece, "core", 1), tuple(result[1]))]

    y_far = fetch(own, 2, 1)
    y = fetch(own, 0, 1)
    up = fetch(own, 1, 0)
    down = fetch(own, 3, 0)
    y_far, y, up, down, first = tie((y_far, y, up, down, first()))
    more_up = fetch(jnp.concatenate([y, up[:half]], axis=0), 1, 0)
    more_down = fetch(jnp.concatenate([y, down[half:]], axis=0), 3, 0)
    early = (
        both(own, (0, 0, 0, rows))
        + both(y, (0, 1, 0, rows))
        + both(up, (1, 0, 0, rows))
        + both(down, (3, 0, 0, rows))
        + both(y_far, (2, 1, 0, rows))
    )
    shape = (16 * rows, own.shape[1])
    more_up, more_down, base, second = tie((more_up, more_down, collect(early, shape), second(y)))
    late = both(more_up, (1, 1, 0, rows), (2, 0, 0, half)) + both(
        more_down, (3, 1, 0, rows), (2, 0, half, half)
    )
    return collect(late, shape, base), first, second


def on_device(activations, residual, w_query, w_key, w_value, w_out, gain, ancestors, kept):
    kv_own = kv_project(activations, w_key, w_value)
    kv, queries, w_held = gather_blocks(
        kv_own,
        lambda: q_project(activations, w_query),
        lambda there: collect([(w_out, ((0, 0, w_out.shape[0]),))], w_out.shape, None, (there,)),
    )

    def send(x, s):
        return shift(x, "tp", s % 4)

    (lo2, hi2), held = block_terms(2, ancestors, queries, kv, w_held)
    a = send(lo2, 1)
    b = send(hi2, 3)
    (lo1, hi1), held = block_terms(1, ancestors, queries, *held)
    u2 = send(hi1, 1)
    (lo3, hi3), held = block_terms(3, ancestors, queries, *held)
    v1 = send(lo3, 3)
    (left, right), _ = block_terms(0, ancestors, queries, *held, residual)
    u1 = send(lo1 + a, 1)
    v2 = send(hi3 + b, 3)
    base = (left + v1.astype(F32), right + u2.astype(F32))
    return final_norm(base, (u1, v2), gain, kept)


def solution(mesh):
    fine = Mesh(mesh.devices.reshape(2, 4, 2, 2, 4), ("dp", "z", "y", "core", "tp"))
    ctx = ("dp",) + CTX
    in_specs = (
        P(ctx, None),
        P(ctx + ("tp",), None),
        P(None, "tp"),
        P(None, "tp"),
        P(None, "tp"),
        P("tp", None),
        P(),
        P(ctx, None),
        P(ctx),
    )
    out_specs = P(ctx + ("tp",), None)
    return jax.shard_map(
        on_device, mesh=fine, in_specs=in_specs, out_specs=out_specs, check_vma=False
    )
```

```python
import functools
import math

import jax
import jax.numpy as jnp
from jax import lax
from jax.experimental import pallas as pl
from jax.experimental.pallas import tpu as pltpu
from jax.sharding import Mesh, PartitionSpec as P

HD = 128
BLK = 128
CHUNK = 4
CTX = ("z", "y", "core")
F32 = jnp.float32
BF16 = jnp.bfloat16
SCALE2 = math.log2(math.e) / math.sqrt(HD)
SPLIT = ((0, 3), (3, 5))
KERNEL_VMEM = 58 << 20
BLOCK_VMEM = 30 << 20
SMALL_COST = pl.CostEstimate(flops=1 << 20, bytes_accessed=1 << 20, transcendentals=0)
NT = (((1,), (1,)), ((), ()))


def kv_kernel(x_ref, wk_ref, wv_ref, o_ref, xbuf, wbuf, sems):
    parts, tile, _ = wbuf.shape
    copies = []
    for k in range(parts):
        cut = pl.ds(k * tile, tile)
        group = [
            pltpu.make_async_copy(x_ref.at[:, cut], xbuf.at[:, cut], sems.at[0, k]),
            pltpu.make_async_copy(wk_ref.at[cut], wbuf.at[k, :, pl.ds(0, HD)], sems.at[1, k]),
            pltpu.make_async_copy(wv_ref.at[cut], wbuf.at[k, :, pl.ds(HD, HD)], sems.at[2, k]),
        ]
        for copy in group:
            copy.start()
        copies.append(group)
    total = None
    for k in range(parts):
        for copy in copies[k]:
            copy.wait()
        part = jnp.dot(
            xbuf[:, k * tile:(k + 1) * tile], wbuf[k], preferred_element_type=F32
        )
        total = part if total is None else total + part
    o_ref[...] = total.astype(BF16)


def kv_project(x, wk, wv):
    rows, depth = x.shape
    parts = 5
    hbm = pl.BlockSpec(memory_space=pltpu.HBM)
    return pl.pallas_call(
        kv_kernel,
        name="kv_project",
        out_shape=jax.ShapeDtypeStruct((rows, 2 * HD), BF16),
        in_specs=[hbm] * 3,
        out_specs=pl.BlockSpec(memory_space=pltpu.VMEM),
        scratch_shapes=[
            pltpu.VMEM((rows, depth), BF16),
            pltpu.VMEM((parts, depth // parts, 2 * HD), BF16),
            pltpu.SemaphoreType.DMA((3, parts)),
        ],
        compiler_params=pltpu.CompilerParams(vmem_limit_bytes=KERNEL_VMEM),
        cost_estimate=SMALL_COST,
    )(x, wk, wv)


def q_kernel(x_ref, w_ref, after_ref, o_ref, wbuf, sems):
    parts, tile, _ = wbuf.shape
    copies = [
        pltpu.make_async_copy(w_ref.at[pl.ds(k * tile, tile)], wbuf.at[k], sems.at[k])
        for k in range(parts)
    ]
    for copy in copies:
        copy.start()
    total = None
    for k in range(parts):
        copies[k].wait()
        part = jnp.dot(x_ref[:, k * tile:(k + 1) * tile], wbuf[k], preferred_element_type=F32)
        total = part if total is None else total + part
    o_ref[...] = total.astype(BF16)


def q_project(x, w, after):
    parts = 5
    vmem = pl.BlockSpec(memory_space=pltpu.VMEM)
    return pl.pallas_call(
        q_kernel,
        name="q_project",
        out_shape=jax.ShapeDtypeStruct((x.shape[0], w.shape[1]), BF16),
        in_specs=[vmem, pl.BlockSpec(memory_space=pltpu.HBM), pl.BlockSpec(memory_space=pl.ANY)],
        out_specs=vmem,
        scratch_shapes=[
            pltpu.VMEM((parts, w.shape[0] // parts, w.shape[1]), BF16),
            pltpu.SemaphoreType.DMA((parts,)),
        ],
        compiler_params=pltpu.CompilerParams(vmem_limit_bytes=20 << 20),
        cost_estimate=SMALL_COST,
    )(x, w, after)


def tie(values):
    spec = pl.BlockSpec(memory_space=pl.ANY)
    return pl.pallas_call(
        lambda *refs: None,
        name="tie",
        out_shape=[jax.ShapeDtypeStruct(x.shape, x.dtype) for x in values],
        in_specs=[spec] * len(values),
        out_specs=[spec] * len(values),
        input_output_aliases={k: k for k in range(len(values))},
        compiler_params=pltpu.CompilerParams(vmem_limit_bytes=1 << 20),
        cost_estimate=SMALL_COST,
    )(*values)


def collect_kernel(moves, based, *refs):
    pieces, out, sems = refs[based:based + len(moves)], refs[-2], refs[-1]
    copies = []
    for piece, cuts in zip(pieces, moves):
        for source, target, size in cuts:
            copies.append(
                pltpu.make_async_copy(
                    piece.at[pl.ds(source, size)],
                    out.at[pl.ds(target, size)],
                    sems.at[len(copies)],
                )
            )
    for copy in copies:
        copy.start()
    for copy in copies:
        copy.wait()


def collect(parts, shape, base=None, after=()):
    pieces, moves = zip(*parts)
    based = 0 if base is None else 1
    return pl.pallas_call(
        functools.partial(collect_kernel, moves, based),
        name="collect",
        out_shape=jax.ShapeDtypeStruct(shape, BF16),
        in_specs=[pl.BlockSpec(memory_space=pl.ANY)] * (based + len(pieces) + len(after)),
        out_specs=pl.BlockSpec(memory_space=pl.ANY),
        scratch_shapes=[pltpu.SemaphoreType.DMA((sum(len(x) for x in moves),))],
        input_output_aliases={0: 0} if based else {},
        compiler_params=pltpu.CompilerParams(vmem_limit_bytes=2 << 20),
        cost_estimate=SMALL_COST,
    )(*([base] if based else []), *pieces, *after)


def attend(q, kv_ref, own_row, rows, count):
    slots = len(rows)
    take = [kv_ref[pl.ds(pl.multiple_of(r, BLK), BLK), :] for r in rows]
    own = kv_ref[pl.ds(pl.multiple_of(own_row, BLK), BLK), :]
    groups = [take[c:c + CHUNK] for c in range(0, slots, CHUNK)]
    keys = [jnp.concatenate([x[:, :HD] for x in g], axis=0) for g in groups]
    values = [jnp.concatenate([x[:, HD:] for x in g], axis=0) for g in groups]
    results = []
    for lo, hi in SPLIT:
        part = q[lo * BLK:hi * BLK]
        s = lax.dot_general(part, own[:, :HD], NT, preferred_element_type=F32)
        row = lax.broadcasted_iota(jnp.int32, s.shape, 0) % BLK
        col = lax.broadcasted_iota(jnp.int32, s.shape, 1)
        pieces = [jnp.where(col <= row, s, -jnp.inf)]
        for c, key in enumerate(keys):
            s = lax.dot_general(part, key, NT, preferred_element_type=F32)
            for j in range(CHUNK):
                pieces.append(
                    jnp.where(c * CHUNK + j < count, s[:, j * BLK:(j + 1) * BLK], -jnp.inf)
                )
        top = pieces[0]
        for piece in pieces[1:]:
            top = jnp.maximum(top, piece)
        top = jnp.max(top, axis=1, keepdims=True)
        weights = [jnp.exp2((piece - top) * SCALE2) for piece in pieces]
        total = weights[0]
        for w in weights[1:]:
            total = total + w
        out = jnp.dot(weights[0].astype(BF16), own[:, HD:], preferred_element_type=F32)
        for c, value in enumerate(values):
            w = jnp.concatenate(
                [x.astype(BF16) for x in weights[1 + c * CHUNK:1 + (c + 1) * CHUNK]], axis=1
            )
            out = out + jnp.dot(w, value, preferred_element_type=F32)
        out = (out / jnp.sum(total, axis=1, keepdims=True)).astype(BF16)
        results += [out[h * BLK:(h + 1) * BLK] for h in range(hi - lo)]
    return jnp.concatenate(results, axis=1)


def block_row(entry, per):
    owner = entry // per
    dz = (owner // 4 - lax.axis_index("z") + 4) % 4
    dy = (owner // 2 + lax.axis_index("y")) % 2
    dc = (owner + lax.axis_index("core")) % 2
    return ((dz * 4 + dy * 2 + dc) * per + entry % per) * BLK


def block_kernel(turn, anc_ref, q_ref, kv_ref, w_ref, *rest):
    res_ref, outs = (rest[0], rest[1:3]) if len(rest) % 2 else (None, rest[:2])
    per, slots = anc_ref.shape
    local = (lax.axis_index("tp") + turn) % per
    rows, count = [], jnp.int32(0)
    for l in range(slots):
        entry = anc_ref[local, l]
        count += jnp.where(entry >= 0, 1, 0).astype(jnp.int32)
        rows.append(block_row(jnp.maximum(entry, 0), per))
    q_all = q_ref[pl.ds(pl.multiple_of(local * BLK, BLK), BLK), :]
    heads = q_all.shape[1] // HD
    q = jnp.concatenate([q_all[:, h * HD:(h + 1) * HD] for h in range(heads)], axis=0)
    head_out = attend(q, kv_ref, local * BLK, rows, count)
    half = outs[0].shape[1]
    tile = half // 2
    for side in range(2):
        for c in range(0, half, tile):
            cut = slice(side * half + c, side * half + c + tile)
            part = jnp.dot(head_out, w_ref[:, cut], preferred_element_type=F32).astype(BF16)
            if res_ref is not None:
                part = part.astype(F32) + res_ref[:, cut].astype(F32)
            outs[side][:, c:c + tile] = part


def block_terms(turn, ancestors, q, kv, w_out, residual=None):
    cols = w_out.shape[1]
    vmem = pl.BlockSpec(memory_space=pltpu.VMEM)
    extra = [] if residual is None else [residual]
    kind = BF16 if residual is None else F32
    outs = pl.pallas_call(
        functools.partial(block_kernel, turn),
        name="block_terms",
        out_shape=[jax.ShapeDtypeStruct((BLK, cols // 2), kind)] * 2
        + [jax.ShapeDtypeStruct(x.shape, x.dtype) for x in (kv, w_out)],
        in_specs=[pl.BlockSpec(memory_space=pltpu.SMEM)] + [vmem] * (3 + len(extra)),
        out_specs=[vmem] * 2 + [pl.BlockSpec(memory_space=pl.ANY)] * 2,
        input_output_aliases={2: 2, 3: 3},
        compiler_params=pltpu.CompilerParams(vmem_limit_bytes=BLOCK_VMEM),
        cost_estimate=SMALL_COST,
    )(ancestors, q, kv, w_out, *extra)
    return outs[:2], outs[2:]


def norm_kernel(b1_ref, b2_ref, u_ref, v_ref, gain_ref, keep_ref, o_ref):
    half = u_ref.shape[1]
    total = [b1_ref[...] + u_ref[...].astype(F32), b2_ref[...] + v_ref[...].astype(F32)]
    square = sum(jnp.sum(x * x, axis=1, keepdims=True) for x in total)
    factor = lax.rsqrt(square * (1.0 / (2 * half)) + 1e-06) * keep_ref[lax.axis_index("tp")].astype(F32)
    for lo, x in zip((0, half), total):
        o_ref[:, lo:lo + half] = (x * factor * gain_ref[:, lo:lo + half]).astype(BF16)


def final_norm(base, last, gain, keep):
    rows, half = base[0].shape
    vm = pl.BlockSpec(memory_space=pltpu.VMEM)
    return pl.pallas_call(
        norm_kernel,
        name="final_norm",
        out_shape=jax.ShapeDtypeStruct((rows, 2 * half), BF16),
        in_specs=[vm] * 5 + [pl.BlockSpec(memory_space=pltpu.SMEM)],
        out_specs=vm,
        compiler_params=pltpu.CompilerParams(vmem_limit_bytes=30 << 20),
    )(*base, *last, gain[None, :], keep)


def ring(n, s):
    return [(i, (i + s) % n) for i in range(n)]


def shift(x, axis, s):
    return lax.ppermute(x, axis, ring({"y": 2, "core": 2, "z": 4, "tp": 4}[axis], s))


def gather_blocks(own, first, second):
    rows = own.shape[0]
    half = rows // 2

    def fetch(x, dz, dy):
        pairs = [(i, ((i // 2 - dz) % 4) * 2 + (i + dy) % 2) for i in range(8)]
        return lax.ppermute(x, ("z", "y"), pairs)

    def both(piece, *moves):
        result, source = ([], []), 0
        for dz, dy, skip, size in moves:
            spot = (dz * 4 + dy * 2) * rows + skip
            for core in range(2):
                result[core].append((source, spot + core * rows, size))
            source += size
        return [(piece, tuple(result[0])), (shift(piece, "core", 1), tuple(result[1]))]

    y_far = fetch(own, 2, 1)
    y = fetch(own, 0, 1)
    up = fetch(own, 1, 0)
    down = fetch(own, 3, 0)
    more_up = fetch(jnp.concatenate([y, up[:half]], axis=0), 1, 0)
    more_down = fetch(jnp.concatenate([y, down[half:]], axis=0), 3, 0)
    y_far, first, second = tie((y_far, first(y), second(y)))
    early = (
        both(own, (0, 0, 0, rows))
        + both(y, (0, 1, 0, rows))
        + both(up, (1, 0, 0, rows))
        + both(down, (3, 0, 0, rows))
        + both(y_far, (2, 1, 0, rows))
    )
    shape = (16 * rows, own.shape[1])
    more_up, more_down, base, first, second = tie(
        (more_up, more_down, collect(early, shape), first, second)
    )
    late = both(more_up, (1, 1, 0, rows), (2, 0, 0, half)) + both(
        more_down, (3, 1, 0, rows), (2, 0, half, half)
    )
    return collect(late, shape, base), first, second


def on_device(activations, residual, w_query, w_key, w_value, w_out, gain, ancestors, kept):
    kv_own = kv_project(activations, w_key, w_value)
    kv, queries, w_held = gather_blocks(
        kv_own,
        lambda there: q_project(activations, w_query, there),
        lambda there: collect([(w_out, ((0, 0, w_out.shape[0]),))], w_out.shape, None, (there,)),
    )

    def send(x, s):
        return shift(x, "tp", s % 4)

    (lo2, hi2), held = block_terms(2, ancestors, queries, kv, w_held)
    a = send(lo2, 1)
    b = send(hi2, 3)
    (lo1, hi1), held = block_terms(1, ancestors, queries, *held)
    u2 = send(hi1, 1)
    (lo3, hi3), held = block_terms(3, ancestors, queries, *held)
    v1 = send(lo3, 3)
    (left, right), _ = block_terms(0, ancestors, queries, *held, residual)
    u1 = send(lo1 + a, 1)
    v2 = send(hi3 + b, 3)
    base = (left + v1.astype(F32), right + u2.astype(F32))
    return final_norm(base, (u1, v2), gain, kept)


def solution(mesh):
    fine = Mesh(mesh.devices.reshape(2, 4, 2, 2, 4), ("dp", "z", "y", "core", "tp"))
    ctx = ("dp",) + CTX
    in_specs = (
        P(ctx, None),
        P(ctx + ("tp",), None),
        P(None, "tp"),
        P(None, "tp"),
        P(None, "tp"),
        P("tp", None),
        P(),
        P(ctx, None),
        P(ctx),
    )
    out_specs = P(ctx + ("tp",), None)
    return jax.shard_map(
        on_device, mesh=fine, in_specs=in_specs, out_specs=out_specs, check_vma=False
    )
```

```python
import functools
import math

import jax
import jax.numpy as jnp
from jax import lax
from jax.experimental import pallas as pl
from jax.experimental.pallas import tpu as pltpu
from jax.sharding import Mesh, PartitionSpec as P

HD = 128
BLK = 128
CHUNK = 4
CTX = ("z", "y", "core")
F32 = jnp.float32
BF16 = jnp.bfloat16
SCALE2 = math.log2(math.e) / math.sqrt(HD)
SPLIT = ((0, 3), (3, 5))
KERNEL_VMEM = 58 << 20
BLOCK_VMEM = 30 << 20
SMALL_COST = pl.CostEstimate(flops=1 << 20, bytes_accessed=1 << 20, transcendentals=0)
NT = (((1,), (1,)), ((), ()))


def kv_kernel(x_ref, wk_ref, wv_ref, o_ref, xbuf, wbuf, sems):
    parts, tile, _ = wbuf.shape
    copies = []
    for k in range(parts):
        cut = pl.ds(k * tile, tile)
        group = [
            pltpu.make_async_copy(x_ref.at[:, cut], xbuf.at[:, cut], sems.at[0, k]),
            pltpu.make_async_copy(wk_ref.at[cut], wbuf.at[k, :, pl.ds(0, HD)], sems.at[1, k]),
            pltpu.make_async_copy(wv_ref.at[cut], wbuf.at[k, :, pl.ds(HD, HD)], sems.at[2, k]),
        ]
        for copy in group:
            copy.start()
        copies.append(group)
    total = None
    for k in range(parts):
        for copy in copies[k]:
            copy.wait()
        part = jnp.dot(
            xbuf[:, k * tile:(k + 1) * tile], wbuf[k], preferred_element_type=F32
        )
        total = part if total is None else total + part
    o_ref[...] = total.astype(BF16)


def kv_project(x, wk, wv):
    rows, depth = x.shape
    parts = 5
    hbm = pl.BlockSpec(memory_space=pltpu.HBM)
    return pl.pallas_call(
        kv_kernel,
        name="kv_project",
        out_shape=jax.ShapeDtypeStruct((rows, 2 * HD), BF16),
        in_specs=[hbm] * 3,
        out_specs=pl.BlockSpec(memory_space=pltpu.VMEM),
        scratch_shapes=[
            pltpu.VMEM((rows, depth), BF16),
            pltpu.VMEM((parts, depth // parts, 2 * HD), BF16),
            pltpu.SemaphoreType.DMA((3, parts)),
        ],
        compiler_params=pltpu.CompilerParams(vmem_limit_bytes=KERNEL_VMEM),
        cost_estimate=SMALL_COST,
    )(x, wk, wv)


def q_kernel(x_ref, w_ref, after_ref, o_ref, wbuf, sems):
    parts, tile, _ = wbuf.shape
    copies = [
        pltpu.make_async_copy(w_ref.at[pl.ds(k * tile, tile)], wbuf.at[k], sems.at[k])
        for k in range(parts)
    ]
    for copy in copies:
        copy.start()
    total = None
    for k in range(parts):
        copies[k].wait()
        part = jnp.dot(x_ref[:, k * tile:(k + 1) * tile], wbuf[k], preferred_element_type=F32)
        total = part if total is None else total + part
    o_ref[...] = total.astype(BF16)


def q_project(x, w, after):
    parts = 5
    vmem = pl.BlockSpec(memory_space=pltpu.VMEM)
    return pl.pallas_call(
        q_kernel,
        name="q_project",
        out_shape=jax.ShapeDtypeStruct((x.shape[0], w.shape[1]), BF16),
        in_specs=[vmem, pl.BlockSpec(memory_space=pltpu.HBM), pl.BlockSpec(memory_space=pl.ANY)],
        out_specs=vmem,
        scratch_shapes=[
            pltpu.VMEM((parts, w.shape[0] // parts, w.shape[1]), BF16),
            pltpu.SemaphoreType.DMA((parts,)),
        ],
        compiler_params=pltpu.CompilerParams(vmem_limit_bytes=46 << 20),
        cost_estimate=SMALL_COST,
    )(x, w, after)


def tie(values):
    spec = pl.BlockSpec(memory_space=pl.ANY)
    return pl.pallas_call(
        lambda *refs: None,
        name="tie",
        out_shape=[jax.ShapeDtypeStruct(x.shape, x.dtype) for x in values],
        in_specs=[spec] * len(values),
        out_specs=[spec] * len(values),
        input_output_aliases={k: k for k in range(len(values))},
        compiler_params=pltpu.CompilerParams(vmem_limit_bytes=1 << 20),
        cost_estimate=SMALL_COST,
    )(*values)


def collect_kernel(moves, based, *refs):
    pieces, out, sems = refs[based:based + len(moves)], refs[-2], refs[-1]
    copies = []
    for piece, cuts in zip(pieces, moves):
        for source, target, size in cuts:
            copies.append(
                pltpu.make_async_copy(
                    piece.at[pl.ds(source, size)],
                    out.at[pl.ds(target, size)],
                    sems.at[len(copies)],
                )
            )
    for copy in copies:
        copy.start()
    for copy in copies:
        copy.wait()


def collect(parts, shape, base=None, after=()):
    pieces, moves = zip(*parts)
    based = 0 if base is None else 1
    return pl.pallas_call(
        functools.partial(collect_kernel, moves, based),
        name="collect",
        out_shape=jax.ShapeDtypeStruct(shape, BF16),
        in_specs=[pl.BlockSpec(memory_space=pl.ANY)] * (based + len(pieces) + len(after)),
        out_specs=pl.BlockSpec(memory_space=pl.ANY),
        scratch_shapes=[pltpu.SemaphoreType.DMA((sum(len(x) for x in moves),))],
        input_output_aliases={0: 0} if based else {},
        compiler_params=pltpu.CompilerParams(vmem_limit_bytes=2 << 20),
        cost_estimate=SMALL_COST,
    )(*([base] if based else []), *pieces, *after)


def attend(q, kv_ref, own_row, rows, count):
    slots = len(rows)
    take = [kv_ref[pl.ds(pl.multiple_of(r, BLK), BLK), :] for r in rows]
    own = kv_ref[pl.ds(pl.multiple_of(own_row, BLK), BLK), :]
    groups = [take[c:c + CHUNK] for c in range(0, slots, CHUNK)]
    keys = [jnp.concatenate([x[:, :HD] for x in g], axis=0) for g in groups]
    values = [jnp.concatenate([x[:, HD:] for x in g], axis=0) for g in groups]
    results = []
    for lo, hi in SPLIT:
        part = q[lo * BLK:hi * BLK]
        s = lax.dot_general(part, own[:, :HD], NT, preferred_element_type=F32)
        row = lax.broadcasted_iota(jnp.int32, s.shape, 0) % BLK
        col = lax.broadcasted_iota(jnp.int32, s.shape, 1)
        pieces = [jnp.where(col <= row, s, -jnp.inf)]
        for c, key in enumerate(keys):
            s = lax.dot_general(part, key, NT, preferred_element_type=F32)
            for j in range(CHUNK):
                pieces.append(
                    jnp.where(c * CHUNK + j < count, s[:, j * BLK:(j + 1) * BLK], -jnp.inf)
                )
        top = pieces[0]
        for piece in pieces[1:]:
            top = jnp.maximum(top, piece)
        top = jnp.max(top, axis=1, keepdims=True)
        weights = [jnp.exp2((piece - top) * SCALE2) for piece in pieces]
        total = weights[0]
        for w in weights[1:]:
            total = total + w
        out = jnp.dot(weights[0].astype(BF16), own[:, HD:], preferred_element_type=F32)
        for c, value in enumerate(values):
            w = jnp.concatenate(
                [x.astype(BF16) for x in weights[1 + c * CHUNK:1 + (c + 1) * CHUNK]], axis=1
            )
            out = out + jnp.dot(w, value, preferred_element_type=F32)
        out = (out / jnp.sum(total, axis=1, keepdims=True)).astype(BF16)
        results += [out[h * BLK:(h + 1) * BLK] for h in range(hi - lo)]
    return jnp.concatenate(results, axis=1)


def block_row(entry, per):
    owner = entry // per
    dz = (owner // 4 - lax.axis_index("z") + 4) % 4
    dy = (owner // 2 + lax.axis_index("y")) % 2
    dc = (owner + lax.axis_index("core")) % 2
    return ((dz * 4 + dy * 2 + dc) * per + entry % per) * BLK


def block_kernel(turn, anc_ref, q_ref, kv_ref, w_ref, *rest):
    res_ref, outs = (rest[0], rest[1:3]) if len(rest) == 4 else (None, rest[:2])
    per, slots = anc_ref.shape
    local = (lax.axis_index("tp") + turn) % per
    rows, count = [], jnp.int32(0)
    for l in range(slots):
        entry = anc_ref[local, l]
        count += jnp.where(entry >= 0, 1, 0).astype(jnp.int32)
        rows.append(block_row(jnp.maximum(entry, 0), per))
    q_all = q_ref[pl.ds(pl.multiple_of(local * BLK, BLK), BLK), :]
    heads = q_all.shape[1] // HD
    q = jnp.concatenate([q_all[:, h * HD:(h + 1) * HD] for h in range(heads)], axis=0)
    head_out = attend(q, kv_ref, local * BLK, rows, count)
    half = outs[0].shape[1]
    tile = half // 2
    for side in range(2):
        for c in range(0, half, tile):
            cut = slice(side * half + c, side * half + c + tile)
            part = jnp.dot(head_out, w_ref[:, cut], preferred_element_type=F32).astype(BF16)
            if res_ref is not None:
                part = part.astype(F32) + res_ref[:, cut].astype(F32)
            outs[side][:, c:c + tile] = part


def block_terms(turn, ancestors, q, kv, w_out, residual=None):
    cols = w_out.shape[1]
    vmem = pl.BlockSpec(memory_space=pltpu.VMEM)
    extra = [] if residual is None else [residual]
    kind = BF16 if residual is None else F32
    outs = pl.pallas_call(
        functools.partial(block_kernel, turn),
        name="block_terms",
        out_shape=[jax.ShapeDtypeStruct((BLK, cols // 2), kind)] * 2
        + [jax.ShapeDtypeStruct(kv.shape, kv.dtype)],
        in_specs=[pl.BlockSpec(memory_space=pltpu.SMEM)] + [vmem] * (3 + len(extra)),
        out_specs=[vmem] * 2 + [pl.BlockSpec(memory_space=pl.ANY)],
        input_output_aliases={2: 2},
        compiler_params=pltpu.CompilerParams(vmem_limit_bytes=BLOCK_VMEM),
        cost_estimate=SMALL_COST,
    )(ancestors, q, kv, w_out, *extra)
    return outs[:2], outs[2]


def norm_kernel(b1_ref, b2_ref, u_ref, v_ref, gain_ref, keep_ref, o_ref, obuf, sems):
    half = u_ref.shape[1]
    tiles = sems.shape[0]
    size = u_ref.shape[0] // tiles
    keep = keep_ref[lax.axis_index("tp")].astype(F32)
    copies = []
    for k in range(tiles):
        cut = slice(k * size, (k + 1) * size)
        total = [
            b1_ref[cut, :] + u_ref[cut, :].astype(F32),
            b2_ref[cut, :] + v_ref[cut, :].astype(F32),
        ]
        square = sum(jnp.sum(x * x, axis=1, keepdims=True) for x in total)
        factor = lax.rsqrt(square * (1.0 / (2 * half)) + 1e-06) * keep
        for lo, x in zip((0, half), total):
            obuf[cut, lo:lo + half] = (x * factor * gain_ref[:, lo:lo + half]).astype(BF16)
        rows = pl.ds(k * size, size)
        copies.append(pltpu.make_async_copy(obuf.at[rows], o_ref.at[rows], sems.at[k]))
        copies[-1].start()
    for copy in copies:
        copy.wait()


def final_norm(base, last, gain, keep):
    rows, half = base[0].shape
    vm = pl.BlockSpec(memory_space=pltpu.VMEM)
    return pl.pallas_call(
        norm_kernel,
        name="final_norm",
        out_shape=jax.ShapeDtypeStruct((rows, 2 * half), BF16),
        in_specs=[vm] * 5 + [pl.BlockSpec(memory_space=pltpu.SMEM)],
        out_specs=pl.BlockSpec(memory_space=pltpu.HBM),
        scratch_shapes=[pltpu.VMEM((rows, 2 * half), BF16), pltpu.SemaphoreType.DMA((4,))],
        compiler_params=pltpu.CompilerParams(vmem_limit_bytes=30 << 20),
    )(*base, *last, gain[None, :], keep)


def ring(n, s):
    return [(i, (i + s) % n) for i in range(n)]


def shift(x, axis, s):
    return lax.ppermute(x, axis, ring({"y": 2, "core": 2, "z": 4, "tp": 4}[axis], s))


def gather_blocks(own, first):
    rows = own.shape[0]
    half = rows // 2

    def fetch(x, dz, dy):
        pairs = [(i, ((i // 2 - dz) % 4) * 2 + (i + dy) % 2) for i in range(8)]
        return lax.ppermute(x, ("z", "y"), pairs)

    def both(piece, *moves):
        result, source = ([], []), 0
        for dz, dy, skip, size in moves:
            spot = (dz * 4 + dy * 2) * rows + skip
            for core in range(2):
                result[core].append((source, spot + core * rows, size))
            source += size
        return [(piece, tuple(result[0])), (shift(piece, "core", 1), tuple(result[1]))]

    y_far = fetch(own, 2, 1)
    up = fetch(own, 1, 0)
    down = fetch(own, 3, 0)
    y = fetch(own, 0, 1)
    more_up = fetch(jnp.concatenate([y, up[:half]], axis=0), 1, 0)
    more_down = fetch(jnp.concatenate([y, down[half:]], axis=0), 3, 0)
    y_far, first = tie((y_far, first(y)))
    early = (
        both(own, (0, 0, 0, rows))
        + both(y, (0, 1, 0, rows))
        + both(up, (1, 0, 0, rows))
        + both(down, (3, 0, 0, rows))
        + both(y_far, (2, 1, 0, rows))
    )
    shape = (16 * rows, own.shape[1])
    more_up, more_down, base, first = tie((more_up, more_down, collect(early, shape), first))
    late = both(more_up, (1, 1, 0, rows), (2, 0, 0, half)) + both(
        more_down, (3, 1, 0, rows), (2, 0, half, half)
    )
    return collect(late, shape, base), first


def on_device(activations, residual, w_query, w_key, w_value, w_out, gain, ancestors, kept):
    kv_own = kv_project(activations, w_key, w_value)
    kv, queries = gather_blocks(kv_own, lambda there: q_project(activations, w_query, there))

    def send(x, s):
        return shift(x, "tp", s % 4)

    (lo2, hi2), kv = block_terms(2, ancestors, queries, kv, w_out)
    a = send(lo2, 1)
    b = send(hi2, 3)
    (lo1, hi1), kv = block_terms(1, ancestors, queries, kv, w_out)
    u2 = send(hi1, 1)
    (lo3, hi3), kv = block_terms(3, ancestors, queries, kv, w_out)
    v1 = send(lo3, 3)
    (left, right), _ = block_terms(0, ancestors, queries, kv, w_out, residual)
    u1 = send(lo1 + a, 1)
    v2 = send(hi3 + b, 3)
    base = (left + v1.astype(F32), right + u2.astype(F32))
    return final_norm(base, (u1, v2), gain, kept)


def solution(mesh):
    fine = Mesh(mesh.devices.reshape(2, 4, 2, 2, 4), ("dp", "z", "y", "core", "tp"))
    ctx = ("dp",) + CTX
    in_specs = (
        P(ctx, None),
        P(ctx + ("tp",), None),
        P(None, "tp"),
        P(None, "tp"),
        P(None, "tp"),
        P("tp", None),
        P(),
        P(ctx, None),
        P(ctx),
    )
    out_specs = P(ctx + ("tp",), None)
    return jax.shard_map(
        on_device, mesh=fine, in_specs=in_specs, out_specs=out_specs, check_vma=False
    )
```

```python
import functools
import math

import jax
import jax.numpy as jnp
from jax import lax
from jax.experimental import pallas as pl
from jax.experimental.pallas import tpu as pltpu
from jax.sharding import Mesh, PartitionSpec as P

HD = 128
BLK = 128
CHUNK = 8
CTX = ("z", "y", "core")
F32 = jnp.float32
BF16 = jnp.bfloat16
SCALE2 = math.log2(math.e) / math.sqrt(HD)
SPLIT = ((0, 3), (3, 5))
KERNEL_VMEM = 58 << 20
BLOCK_VMEM = 30 << 20
SMALL_COST = pl.CostEstimate(flops=1 << 20, bytes_accessed=1 << 20, transcendentals=0)
NT = (((1,), (1,)), ((), ()))


def kv_kernel(x_ref, wk_ref, wv_ref, o_ref, xbuf, wbuf, sems):
    parts, tile, _ = wbuf.shape
    copies = []
    for k in range(parts):
        cut = pl.ds(k * tile, tile)
        group = [
            pltpu.make_async_copy(x_ref.at[:, cut], xbuf.at[:, cut], sems.at[0, k]),
            pltpu.make_async_copy(wk_ref.at[cut], wbuf.at[k, :, pl.ds(0, HD)], sems.at[1, k]),
            pltpu.make_async_copy(wv_ref.at[cut], wbuf.at[k, :, pl.ds(HD, HD)], sems.at[2, k]),
        ]
        for copy in group:
            copy.start()
        copies.append(group)
    total = None
    for k in range(parts):
        for copy in copies[k]:
            copy.wait()
        part = jnp.dot(
            xbuf[:, k * tile:(k + 1) * tile], wbuf[k], preferred_element_type=F32
        )
        total = part if total is None else total + part
    o_ref[...] = total.astype(BF16)


def kv_project(x, wk, wv):
    rows, depth = x.shape
    parts = 5
    hbm = pl.BlockSpec(memory_space=pltpu.HBM)
    return pl.pallas_call(
        kv_kernel,
        name="kv_project",
        out_shape=jax.ShapeDtypeStruct((rows, 2 * HD), BF16),
        in_specs=[hbm] * 3,
        out_specs=pl.BlockSpec(memory_space=pltpu.VMEM),
        scratch_shapes=[
            pltpu.VMEM((rows, depth), BF16),
            pltpu.VMEM((parts, depth // parts, 2 * HD), BF16),
            pltpu.SemaphoreType.DMA((3, parts)),
        ],
        compiler_params=pltpu.CompilerParams(vmem_limit_bytes=KERNEL_VMEM),
        cost_estimate=SMALL_COST,
    )(x, wk, wv)


def q_kernel(x_ref, w_ref, after_ref, o_ref, wbuf, sems):
    parts, tile, _ = wbuf.shape
    copies = [
        pltpu.make_async_copy(w_ref.at[pl.ds(k * tile, tile)], wbuf.at[k], sems.at[k])
        for k in range(parts)
    ]
    for copy in copies:
        copy.start()
    total = None
    for k in range(parts):
        copies[k].wait()
        part = jnp.dot(x_ref[:, k * tile:(k + 1) * tile], wbuf[k], preferred_element_type=F32)
        total = part if total is None else total + part
    o_ref[...] = total.astype(BF16)


def q_project(x, w, after):
    parts = 5
    vmem = pl.BlockSpec(memory_space=pltpu.VMEM)
    return pl.pallas_call(
        q_kernel,
        name="q_project",
        out_shape=jax.ShapeDtypeStruct((x.shape[0], w.shape[1]), BF16),
        in_specs=[vmem, pl.BlockSpec(memory_space=pltpu.HBM), pl.BlockSpec(memory_space=pl.ANY)],
        out_specs=vmem,
        scratch_shapes=[
            pltpu.VMEM((parts, w.shape[0] // parts, w.shape[1]), BF16),
            pltpu.SemaphoreType.DMA((parts,)),
        ],
        compiler_params=pltpu.CompilerParams(vmem_limit_bytes=46 << 20),
        cost_estimate=SMALL_COST,
    )(x, w, after)


def tie(values):
    spec = pl.BlockSpec(memory_space=pl.ANY)
    return pl.pallas_call(
        lambda *refs: None,
        name="tie",
        out_shape=[jax.ShapeDtypeStruct(x.shape, x.dtype) for x in values],
        in_specs=[spec] * len(values),
        out_specs=[spec] * len(values),
        input_output_aliases={k: k for k in range(len(values))},
        compiler_params=pltpu.CompilerParams(vmem_limit_bytes=1 << 20),
        cost_estimate=SMALL_COST,
    )(*values)


def collect_kernel(moves, based, *refs):
    pieces, out, sems = refs[based:based + len(moves)], refs[-2], refs[-1]
    copies = []
    for piece, cuts in zip(pieces, moves):
        for source, target, size in cuts:
            copies.append(
                pltpu.make_async_copy(
                    piece.at[pl.ds(source, size)],
                    out.at[pl.ds(target, size)],
                    sems.at[len(copies)],
                )
            )
    for copy in copies:
        copy.start()
    for copy in copies:
        copy.wait()


def collect(parts, shape, base=None, after=()):
    pieces, moves = zip(*parts)
    based = 0 if base is None else 1
    return pl.pallas_call(
        functools.partial(collect_kernel, moves, based),
        name="collect",
        out_shape=jax.ShapeDtypeStruct(shape, BF16),
        in_specs=[pl.BlockSpec(memory_space=pl.ANY)] * (based + len(pieces) + len(after)),
        out_specs=pl.BlockSpec(memory_space=pl.ANY),
        scratch_shapes=[pltpu.SemaphoreType.DMA((sum(len(x) for x in moves),))],
        input_output_aliases={0: 0} if based else {},
        compiler_params=pltpu.CompilerParams(vmem_limit_bytes=2 << 20),
        cost_estimate=SMALL_COST,
    )(*([base] if based else []), *pieces, *after)


def attend(q, kv_ref, own_row, rows, count):
    slots = len(rows)
    take = [kv_ref[pl.ds(pl.multiple_of(r, BLK), BLK), :] for r in rows]
    own = kv_ref[pl.ds(pl.multiple_of(own_row, BLK), BLK), :]
    groups = [take[c:c + CHUNK] for c in range(0, slots, CHUNK)]
    keys = [jnp.concatenate([x[:, :HD] for x in g], axis=0) for g in groups]
    values = [jnp.concatenate([x[:, HD:] for x in g], axis=0) for g in groups]
    results = []
    for lo, hi in SPLIT:
        part = q[lo * BLK:hi * BLK]
        s = lax.dot_general(part, own[:, :HD], NT, preferred_element_type=F32)
        row = lax.broadcasted_iota(jnp.int32, s.shape, 0) % BLK
        col = lax.broadcasted_iota(jnp.int32, s.shape, 1)
        pieces = [jnp.where(col <= row, s, -jnp.inf)]
        for c, key in enumerate(keys):
            s = lax.dot_general(part, key, NT, preferred_element_type=F32)
            for j in range(CHUNK):
                pieces.append(
                    jnp.where(c * CHUNK + j < count, s[:, j * BLK:(j + 1) * BLK], -jnp.inf)
                )
        top = pieces[0]
        for piece in pieces[1:]:
            top = jnp.maximum(top, piece)
        top = jnp.max(top, axis=1, keepdims=True)
        weights = [jnp.exp2((piece - top) * SCALE2) for piece in pieces]
        total = weights[0]
        for w in weights[1:]:
            total = total + w
        out = jnp.dot(weights[0].astype(BF16), own[:, HD:], preferred_element_type=F32)
        for c, value in enumerate(values):
            w = jnp.concatenate(
                [x.astype(BF16) for x in weights[1 + c * CHUNK:1 + (c + 1) * CHUNK]], axis=1
            )
            out = out + jnp.dot(w, value, preferred_element_type=F32)
        out = (out / jnp.sum(total, axis=1, keepdims=True)).astype(BF16)
        results += [out[h * BLK:(h + 1) * BLK] for h in range(hi - lo)]
    return jnp.concatenate(results, axis=1)


def block_row(entry, per):
    owner = entry // per
    dz = (owner // 4 - lax.axis_index("z") + 4) % 4
    dy = (owner // 2 + lax.axis_index("y")) % 2
    dc = (owner + lax.axis_index("core")) % 2
    return ((dz * 4 + dy * 2 + dc) * per + entry % per) * BLK


def block_kernel(turn, anc_ref, q_ref, kv_ref, w_ref, *rest):
    res_ref, outs = (rest[0], rest[1:3]) if len(rest) == 4 else (None, rest[:2])
    per, slots = anc_ref.shape
    local = (lax.axis_index("tp") + turn) % per
    rows, count = [], jnp.int32(0)
    for l in range(slots):
        entry = anc_ref[local, l]
        count += jnp.where(entry >= 0, 1, 0).astype(jnp.int32)
        rows.append(block_row(jnp.maximum(entry, 0), per))
    q_all = q_ref[pl.ds(pl.multiple_of(local * BLK, BLK), BLK), :]
    heads = q_all.shape[1] // HD
    q = jnp.concatenate([q_all[:, h * HD:(h + 1) * HD] for h in range(heads)], axis=0)
    head_out = attend(q, kv_ref, local * BLK, rows, count)
    half = outs[0].shape[1]
    tile = half // 2
    for side in range(2):
        for c in range(0, half, tile):
            cut = slice(side * half + c, side * half + c + tile)
            part = jnp.dot(head_out, w_ref[:, cut], preferred_element_type=F32).astype(BF16)
            if res_ref is not None:
                part = part.astype(F32) + res_ref[:, cut].astype(F32)
            outs[side][:, c:c + tile] = part


def block_terms(turn, ancestors, q, kv, w_out, residual=None):
    cols = w_out.shape[1]
    vmem = pl.BlockSpec(memory_space=pltpu.VMEM)
    extra = [] if residual is None else [residual]
    kind = BF16 if residual is None else F32
    outs = pl.pallas_call(
        functools.partial(block_kernel, turn),
        name="block_terms",
        out_shape=[jax.ShapeDtypeStruct((BLK, cols // 2), kind)] * 2
        + [jax.ShapeDtypeStruct(kv.shape, kv.dtype)],
        in_specs=[pl.BlockSpec(memory_space=pltpu.SMEM)] + [vmem] * (3 + len(extra)),
        out_specs=[vmem] * 2 + [pl.BlockSpec(memory_space=pl.ANY)],
        input_output_aliases={2: 2},
        compiler_params=pltpu.CompilerParams(vmem_limit_bytes=BLOCK_VMEM),
        cost_estimate=SMALL_COST,
    )(ancestors, q, kv, w_out, *extra)
    return outs[:2], outs[2]


def norm_kernel(b1_ref, b2_ref, u_ref, v_ref, gain_ref, keep_ref, o_ref, obuf, sems):
    half = u_ref.shape[1]
    tiles = sems.shape[0]
    size = u_ref.shape[0] // tiles
    keep = keep_ref[lax.axis_index("tp")].astype(F32)
    copies = []
    for k in range(tiles):
        cut = slice(k * size, (k + 1) * size)
        total = [
            b1_ref[cut, :] + u_ref[cut, :].astype(F32),
            b2_ref[cut, :] + v_ref[cut, :].astype(F32),
        ]
        square = sum(jnp.sum(x * x, axis=1, keepdims=True) for x in total)
        factor = lax.rsqrt(square * (1.0 / (2 * half)) + 1e-06) * keep
        for lo, x in zip((0, half), total):
            obuf[cut, lo:lo + half] = (x * factor * gain_ref[:, lo:lo + half]).astype(BF16)
        rows = pl.ds(k * size, size)
        copies.append(pltpu.make_async_copy(obuf.at[rows], o_ref.at[rows], sems.at[k]))
        copies[-1].start()
    for copy in copies:
        copy.wait()


def final_norm(base, last, gain, keep):
    rows, half = base[0].shape
    vm = pl.BlockSpec(memory_space=pltpu.VMEM)
    return pl.pallas_call(
        norm_kernel,
        name="final_norm",
        out_shape=jax.ShapeDtypeStruct((rows, 2 * half), BF16),
        in_specs=[vm] * 5 + [pl.BlockSpec(memory_space=pltpu.SMEM)],
        out_specs=pl.BlockSpec(memory_space=pltpu.HBM),
        scratch_shapes=[pltpu.VMEM((rows, 2 * half), BF16), pltpu.SemaphoreType.DMA((4,))],
        compiler_params=pltpu.CompilerParams(vmem_limit_bytes=30 << 20),
    )(*base, *last, gain[None, :], keep)


def ring(n, s):
    return [(i, (i + s) % n) for i in range(n)]


def shift(x, axis, s):
    return lax.ppermute(x, axis, ring({"y": 2, "core": 2, "z": 4, "tp": 4}[axis], s))


def gather_blocks(own, first):
    rows = own.shape[0]
    half = rows // 2

    def fetch(x, dz, dy):
        pairs = [(i, ((i // 2 - dz) % 4) * 2 + (i + dy) % 2) for i in range(8)]
        return lax.ppermute(x, ("z", "y"), pairs)

    def both(piece, *moves):
        result, source = ([], []), 0
        for dz, dy, skip, size in moves:
            spot = (dz * 4 + dy * 2) * rows + skip
            for core in range(2):
                result[core].append((source, spot + core * rows, size))
            source += size
        return [(piece, tuple(result[0])), (shift(piece, "core", 1), tuple(result[1]))]

    y_far = fetch(own, 2, 1)
    up = fetch(own, 1, 0)
    down = fetch(own, 3, 0)
    y = fetch(own, 0, 1)
    more_up = fetch(jnp.concatenate([y, up[:half]], axis=0), 1, 0)
    more_down = fetch(jnp.concatenate([y, down[half:]], axis=0), 3, 0)
    y_far, first = tie((y_far, first(y)))
    early = (
        both(own, (0, 0, 0, rows))
        + both(y, (0, 1, 0, rows))
        + both(up, (1, 0, 0, rows))
        + both(down, (3, 0, 0, rows))
        + both(y_far, (2, 1, 0, rows))
    )
    shape = (16 * rows, own.shape[1])
    more_up, more_down, base, first = tie((more_up, more_down, collect(early, shape), first))
    late = both(more_up, (1, 1, 0, rows), (2, 0, 0, half)) + both(
        more_down, (3, 1, 0, rows), (2, 0, half, half)
    )
    return collect(late, shape, base), first


def on_device(activations, residual, w_query, w_key, w_value, w_out, gain, ancestors, kept):
    kv_own = kv_project(activations, w_key, w_value)
    kv, queries = gather_blocks(kv_own, lambda there: q_project(activations, w_query, there))

    def send(x, s):
        return shift(x, "tp", s % 4)

    (lo2, hi2), kv = block_terms(2, ancestors, queries, kv, w_out)
    a = send(lo2, 1)
    b = send(hi2, 3)
    (lo1, hi1), kv = block_terms(1, ancestors, queries, kv, w_out)
    u2 = send(hi1, 1)
    (lo3, hi3), kv = block_terms(3, ancestors, queries, kv, w_out)
    v1 = send(lo3, 3)
    (left, right), _ = block_terms(0, ancestors, queries, kv, w_out, residual)
    u1 = send(lo1 + a, 1)
    v2 = send(hi3 + b, 3)
    base = (left + v1.astype(F32), right + u2.astype(F32))
    return final_norm(base, (u1, v2), gain, kept)


def solution(mesh):
    fine = Mesh(mesh.devices.reshape(2, 4, 2, 2, 4), ("dp", "z", "y", "core", "tp"))
    ctx = ("dp",) + CTX
    in_specs = (
        P(ctx, None),
        P(ctx + ("tp",), None),
        P(None, "tp"),
        P(None, "tp"),
        P(None, "tp"),
        P("tp", None),
        P(),
        P(ctx, None),
        P(ctx),
    )
    out_specs = P(ctx + ("tp",), None)
    return jax.shard_map(
        on_device, mesh=fine, in_specs=in_specs, out_specs=out_specs, check_vma=False
    )
```

```python
import functools
import math

import jax
import jax.numpy as jnp
from jax import lax
from jax.experimental import pallas as pl
from jax.experimental.pallas import tpu as pltpu
from jax.sharding import Mesh, PartitionSpec as P

HD = 128
BLK = 128
CHUNK = 4
CTX = ("z", "y", "core")
F32 = jnp.float32
BF16 = jnp.bfloat16
SCALE2 = math.log2(math.e) / math.sqrt(HD)
SPLIT = ((0, 3), (3, 5))
KERNEL_VMEM = 58 << 20
BLOCK_VMEM = 30 << 20
SMALL_COST = pl.CostEstimate(flops=1 << 20, bytes_accessed=1 << 20, transcendentals=0)
NT = (((1,), (1,)), ((), ()))


def kv_kernel(x_ref, wk_ref, wv_ref, o_ref, xbuf, wbuf, sems):
    parts, tile, _ = wbuf.shape
    copies = []
    for k in range(parts):
        cut = pl.ds(k * tile, tile)
        group = [
            pltpu.make_async_copy(x_ref.at[:, cut], xbuf.at[:, cut], sems.at[0, k]),
            pltpu.make_async_copy(wk_ref.at[cut], wbuf.at[k, :, pl.ds(0, HD)], sems.at[1, k]),
            pltpu.make_async_copy(wv_ref.at[cut], wbuf.at[k, :, pl.ds(HD, HD)], sems.at[2, k]),
        ]
        for copy in group:
            copy.start()
        copies.append(group)
    total = None
    for k in range(parts):
        for copy in copies[k]:
            copy.wait()
        part = jnp.dot(
            xbuf[:, k * tile:(k + 1) * tile], wbuf[k], preferred_element_type=F32
        )
        total = part if total is None else total + part
    o_ref[...] = total.astype(BF16)


def kv_project(x, wk, wv):
    rows, depth = x.shape
    parts = 2
    hbm = pl.BlockSpec(memory_space=pltpu.HBM)
    return pl.pallas_call(
        kv_kernel,
        name="kv_project",
        out_shape=jax.ShapeDtypeStruct((rows, 2 * HD), BF16),
        in_specs=[hbm] * 3,
        out_specs=pl.BlockSpec(memory_space=pltpu.VMEM),
        scratch_shapes=[
            pltpu.VMEM((rows, depth), BF16),
            pltpu.VMEM((parts, depth // parts, 2 * HD), BF16),
            pltpu.SemaphoreType.DMA((3, parts)),
        ],
        compiler_params=pltpu.CompilerParams(vmem_limit_bytes=KERNEL_VMEM),
        cost_estimate=SMALL_COST,
    )(x, wk, wv)


def q_kernel(x_ref, w_ref, after_ref, o_ref, wbuf, sems):
    parts, tile, _ = wbuf.shape
    copies = [
        pltpu.make_async_copy(w_ref.at[pl.ds(k * tile, tile)], wbuf.at[k], sems.at[k])
        for k in range(parts)
    ]
    for copy in copies:
        copy.start()
    total = None
    for k in range(parts):
        copies[k].wait()
        part = jnp.dot(x_ref[:, k * tile:(k + 1) * tile], wbuf[k], preferred_element_type=F32)
        total = part if total is None else total + part
    o_ref[...] = total.astype(BF16)


def q_project(x, w, after):
    parts = 5
    vmem = pl.BlockSpec(memory_space=pltpu.VMEM)
    return pl.pallas_call(
        q_kernel,
        name="q_project",
        out_shape=jax.ShapeDtypeStruct((x.shape[0], w.shape[1]), BF16),
        in_specs=[vmem, pl.BlockSpec(memory_space=pltpu.HBM), pl.BlockSpec(memory_space=pl.ANY)],
        out_specs=vmem,
        scratch_shapes=[
            pltpu.VMEM((parts, w.shape[0] // parts, w.shape[1]), BF16),
            pltpu.SemaphoreType.DMA((parts,)),
        ],
        compiler_params=pltpu.CompilerParams(vmem_limit_bytes=46 << 20),
        cost_estimate=SMALL_COST,
    )(x, w, after)


def tie(values):
    spec = pl.BlockSpec(memory_space=pl.ANY)
    return pl.pallas_call(
        lambda *refs: None,
        name="tie",
        out_shape=[jax.ShapeDtypeStruct(x.shape, x.dtype) for x in values],
        in_specs=[spec] * len(values),
        out_specs=[spec] * len(values),
        input_output_aliases={k: k for k in range(len(values))},
        compiler_params=pltpu.CompilerParams(vmem_limit_bytes=1 << 20),
        cost_estimate=SMALL_COST,
    )(*values)


def collect_kernel(moves, based, *refs):
    pieces, out, sems = refs[based:based + len(moves)], refs[-2], refs[-1]
    copies = []
    for piece, cuts in zip(pieces, moves):
        for source, target, size in cuts:
            copies.append(
                pltpu.make_async_copy(
                    piece.at[pl.ds(source, size)],
                    out.at[pl.ds(target, size)],
                    sems.at[len(copies)],
                )
            )
    for copy in copies:
        copy.start()
    for copy in copies:
        copy.wait()


def collect(parts, shape, base=None, after=()):
    pieces, moves = zip(*parts)
    based = 0 if base is None else 1
    return pl.pallas_call(
        functools.partial(collect_kernel, moves, based),
        name="collect",
        out_shape=jax.ShapeDtypeStruct(shape, BF16),
        in_specs=[pl.BlockSpec(memory_space=pl.ANY)] * (based + len(pieces) + len(after)),
        out_specs=pl.BlockSpec(memory_space=pl.ANY),
        scratch_shapes=[pltpu.SemaphoreType.DMA((sum(len(x) for x in moves),))],
        input_output_aliases={0: 0} if based else {},
        compiler_params=pltpu.CompilerParams(vmem_limit_bytes=2 << 20),
        cost_estimate=SMALL_COST,
    )(*([base] if based else []), *pieces, *after)


def attend(q, kv_ref, own_row, rows, count):
    slots = len(rows)
    take = [kv_ref[pl.ds(pl.multiple_of(r, BLK), BLK), :] for r in rows]
    own = kv_ref[pl.ds(pl.multiple_of(own_row, BLK), BLK), :]
    groups = [take[c:c + CHUNK] for c in range(0, slots, CHUNK)]
    keys = [jnp.concatenate([x[:, :HD] for x in g], axis=0) for g in groups]
    values = [jnp.concatenate([x[:, HD:] for x in g], axis=0) for g in groups]
    results = []
    for lo, hi in SPLIT:
        part = q[lo * BLK:hi * BLK]
        s = lax.dot_general(part, own[:, :HD], NT, preferred_element_type=F32)
        row = lax.broadcasted_iota(jnp.int32, s.shape, 0) % BLK
        col = lax.broadcasted_iota(jnp.int32, s.shape, 1)
        pieces = [jnp.where(col <= row, s, -jnp.inf)]
        for c, key in enumerate(keys):
            s = lax.dot_general(part, key, NT, preferred_element_type=F32)
            for j in range(CHUNK):
                pieces.append(
                    jnp.where(c * CHUNK + j < count, s[:, j * BLK:(j + 1) * BLK], -jnp.inf)
                )
        top = pieces[0]
        for piece in pieces[1:]:
            top = jnp.maximum(top, piece)
        top = jnp.max(top, axis=1, keepdims=True)
        weights = [jnp.exp2((piece - top) * SCALE2) for piece in pieces]
        total = weights[0]
        for w in weights[1:]:
            total = total + w
        out = jnp.dot(weights[0].astype(BF16), own[:, HD:], preferred_element_type=F32)
        for c, value in enumerate(values):
            w = jnp.concatenate(
                [x.astype(BF16) for x in weights[1 + c * CHUNK:1 + (c + 1) * CHUNK]], axis=1
            )
            out = out + jnp.dot(w, value, preferred_element_type=F32)
        out = (out / jnp.sum(total, axis=1, keepdims=True)).astype(BF16)
        results += [out[h * BLK:(h + 1) * BLK] for h in range(hi - lo)]
    return jnp.concatenate(results, axis=1)


def block_row(entry, per):
    owner = entry // per
    dz = (owner // 4 - lax.axis_index("z") + 4) % 4
    dy = (owner // 2 + lax.axis_index("y")) % 2
    dc = (owner + lax.axis_index("core")) % 2
    return ((dz * 4 + dy * 2 + dc) * per + entry % per) * BLK


def block_kernel(turn, anc_ref, q_ref, kv_ref, w_ref, *rest):
    res_ref, outs = (rest[0], rest[1:3]) if len(rest) == 4 else (None, rest[:2])
    per, slots = anc_ref.shape
    local = (lax.axis_index("tp") + turn) % per
    rows, count = [], jnp.int32(0)
    for l in range(slots):
        entry = anc_ref[local, l]
        count += jnp.where(entry >= 0, 1, 0).astype(jnp.int32)
        rows.append(block_row(jnp.maximum(entry, 0), per))
    q_all = q_ref[pl.ds(pl.multiple_of(local * BLK, BLK), BLK), :]
    heads = q_all.shape[1] // HD
    q = jnp.concatenate([q_all[:, h * HD:(h + 1) * HD] for h in range(heads)], axis=0)
    head_out = attend(q, kv_ref, local * BLK, rows, count)
    half = outs[0].shape[1]
    tile = half // 2
    for side in range(2):
        for c in range(0, half, tile):
            cut = slice(side * half + c, side * half + c + tile)
            part = jnp.dot(head_out, w_ref[:, cut], preferred_element_type=F32).astype(BF16)
            if res_ref is not None:
                part = part.astype(F32) + res_ref[:, cut].astype(F32)
            outs[side][:, c:c + tile] = part


def block_terms(turn, ancestors, q, kv, w_out, residual=None):
    cols = w_out.shape[1]
    vmem = pl.BlockSpec(memory_space=pltpu.VMEM)
    extra = [] if residual is None else [residual]
    kind = BF16 if residual is None else F32
    outs = pl.pallas_call(
        functools.partial(block_kernel, turn),
        name="block_terms",
        out_shape=[jax.ShapeDtypeStruct((BLK, cols // 2), kind)] * 2
        + [jax.ShapeDtypeStruct(kv.shape, kv.dtype)],
        in_specs=[pl.BlockSpec(memory_space=pltpu.SMEM)] + [vmem] * (3 + len(extra)),
        out_specs=[vmem] * 2 + [pl.BlockSpec(memory_space=pl.ANY)],
        input_output_aliases={2: 2},
        compiler_params=pltpu.CompilerParams(vmem_limit_bytes=BLOCK_VMEM),
        cost_estimate=SMALL_COST,
    )(ancestors, q, kv, w_out, *extra)
    return outs[:2], outs[2]


def norm_kernel(b1_ref, b2_ref, u_ref, v_ref, gain_ref, keep_ref, o_ref, obuf, sems):
    half = u_ref.shape[1]
    tiles = sems.shape[0]
    size = u_ref.shape[0] // tiles
    keep = keep_ref[lax.axis_index("tp")].astype(F32)
    copies = []
    for k in range(tiles):
        cut = slice(k * size, (k + 1) * size)
        total = [
            b1_ref[cut, :] + u_ref[cut, :].astype(F32),
            b2_ref[cut, :] + v_ref[cut, :].astype(F32),
        ]
        square = sum(jnp.sum(x * x, axis=1, keepdims=True) for x in total)
        factor = lax.rsqrt(square * (1.0 / (2 * half)) + 1e-06) * keep
        for lo, x in zip((0, half), total):
            obuf[cut, lo:lo + half] = (x * factor * gain_ref[:, lo:lo + half]).astype(BF16)
        rows = pl.ds(k * size, size)
        copies.append(pltpu.make_async_copy(obuf.at[rows], o_ref.at[rows], sems.at[k]))
        copies[-1].start()
    for copy in copies:
        copy.wait()


def final_norm(base, last, gain, keep):
    rows, half = base[0].shape
    vm = pl.BlockSpec(memory_space=pltpu.VMEM)
    return pl.pallas_call(
        norm_kernel,
        name="final_norm",
        out_shape=jax.ShapeDtypeStruct((rows, 2 * half), BF16),
        in_specs=[vm] * 5 + [pl.BlockSpec(memory_space=pltpu.SMEM)],
        out_specs=pl.BlockSpec(memory_space=pltpu.HBM),
        scratch_shapes=[pltpu.VMEM((rows, 2 * half), BF16), pltpu.SemaphoreType.DMA((4,))],
        compiler_params=pltpu.CompilerParams(vmem_limit_bytes=30 << 20),
    )(*base, *last, gain[None, :], keep)


def ring(n, s):
    return [(i, (i + s) % n) for i in range(n)]


def shift(x, axis, s):
    return lax.ppermute(x, axis, ring({"y": 2, "core": 2, "z": 4, "tp": 4}[axis], s))


def gather_blocks(own, first):
    rows = own.shape[0]
    half = rows // 2

    def fetch(x, dz, dy):
        pairs = [(i, ((i // 2 - dz) % 4) * 2 + (i + dy) % 2) for i in range(8)]
        return lax.ppermute(x, ("z", "y"), pairs)

    def both(piece, *moves):
        result, source = ([], []), 0
        for dz, dy, skip, size in moves:
            spot = (dz * 4 + dy * 2) * rows + skip
            for core in range(2):
                result[core].append((source, spot + core * rows, size))
            source += size
        return [(piece, tuple(result[0])), (shift(piece, "core", 1), tuple(result[1]))]

    y_far = fetch(own, 2, 1)
    up = fetch(own, 1, 0)
    down = fetch(own, 3, 0)
    y = fetch(own, 0, 1)
    more_up = fetch(jnp.concatenate([y, up[:half]], axis=0), 1, 0)
    more_down = fetch(jnp.concatenate([y, down[half:]], axis=0), 3, 0)
    y_far, first = tie((y_far, first(y)))
    early = (
        both(own, (0, 0, 0, rows))
        + both(y, (0, 1, 0, rows))
        + both(up, (1, 0, 0, rows))
        + both(down, (3, 0, 0, rows))
        + both(y_far, (2, 1, 0, rows))
    )
    shape = (16 * rows, own.shape[1])
    more_up, more_down, base, first = tie((more_up, more_down, collect(early, shape), first))
    late = both(more_up, (1, 1, 0, rows), (2, 0, 0, half)) + both(
        more_down, (3, 1, 0, rows), (2, 0, half, half)
    )
    return collect(late, shape, base), first


def on_device(activations, residual, w_query, w_key, w_value, w_out, gain, ancestors, kept):
    kv_own = kv_project(activations, w_key, w_value)
    kv, queries = gather_blocks(kv_own, lambda there: q_project(activations, w_query, there))

    def send(x, s):
        return shift(x, "tp", s % 4)

    (lo2, hi2), kv = block_terms(2, ancestors, queries, kv, w_out)
    a = send(lo2, 1)
    b = send(hi2, 3)
    (lo1, hi1), kv = block_terms(1, ancestors, queries, kv, w_out)
    u2 = send(hi1, 1)
    (lo3, hi3), kv = block_terms(3, ancestors, queries, kv, w_out)
    v1 = send(lo3, 3)
    (left, right), _ = block_terms(0, ancestors, queries, kv, w_out, residual)
    u1 = send(lo1 + a, 1)
    v2 = send(hi3 + b, 3)
    base = (left + v1.astype(F32), right + u2.astype(F32))
    return final_norm(base, (u1, v2), gain, kept)


def solution(mesh):
    fine = Mesh(mesh.devices.reshape(2, 4, 2, 2, 4), ("dp", "z", "y", "core", "tp"))
    ctx = ("dp",) + CTX
    in_specs = (
        P(ctx, None),
        P(ctx + ("tp",), None),
        P(None, "tp"),
        P(None, "tp"),
        P(None, "tp"),
        P("tp", None),
        P(),
        P(ctx, None),
        P(ctx),
    )
    out_specs = P(ctx + ("tp",), None)
    return jax.shard_map(
        on_device, mesh=fine, in_specs=in_specs, out_specs=out_specs, check_vma=False
    )
```
